256 devices in a mesh: row: 16 (over z, core), col: 16 (over y, x).
Axes of the slice: x: 4, y: 4, z: 8, core: 2. Of those that a mesh axis runs over, the one named last changes fastest.
Arguments:
- start_block: float32 [4096, 64, 128], P(('row', 'col')), may hold values from -2700 to 2700
- tile_values: bfloat16 [65536, 128, 128], P(('row', 'col')), may hold values from -3.535534 to 3.535534
- tile_rows: int32 [65536], P(('row', 'col')), may hold values from 0 to 15
- tile_cols: int32 [65536], P(('row', 'col')), may hold values from 0 to 79
- tile_count: int32 [256], P(('row', 'col')), may hold values from 32 to 256, as said below
- send_rows: int32 [256, 256, 32], P(('row', 'col')), may hold values from 0 to 2047
- send_count: int32 [256, 256], P(('row', 'col')), may hold values from 16 to 32, as said below
- rotation: float32 [192, 64], replicated, may hold values from -0.4375 to 0.4375
Outputs:
- embedding: float32 [4096, 64, 128], P(('row', 'col'))
The draws below stay inside these ranges and needn't reach their ends.
Inputs may be any that keep to these rules, and one draw needn't show every extreme that they name: `tile_cols`: source tiles below 16 are the partition's own row tiles, the others its halo tiles. `tile_count`: slots at or past the count are ignored; some partition fills all 256 slots. `send_count`: slots at or past the count carry zeros; every partition fills all 32 slots for some peer, and some partition receives 32 rows from every partition.
All inputs are finite; a program needn't handle non-finite values.
Results may differ from the reference program's by a relative error of at most 0.0029.
Values may be sent and summed in bfloat16 or wider, within the bound.
A program may use at most 64 MiB of HBM per device.

```python
import math
import jax
import jax.numpy as jnp
from jax import lax

BLK = 64
TILE = 128
TPR = 16
RT = 16
CAP = 32
DEVS = 256
NT = 256
ROWS_DEV = 2048
ROW_TILES = 4096
NODES = 524288
HALO_TILES = 64
SRC_TILES = 80
BASIS = 192


def device_trend(count, per_device, factor):
    position = jnp.arange(count * per_device, dtype=jnp.int32) // per_device
    return jnp.exp(math.log(factor) * position.astype(jnp.float32) / max(count - 1, 1))


def draw_start_block(key, part):
    keys = jax.random.split(jax.random.fold_in(key, 11), 3)
    shape = (ROW_TILES, BLK, TILE)
    row_scale = jnp.exp(jax.random.uniform(keys[0], (ROW_TILES, 1, TILE), minval=0.0, maxval=math.log(10.0)))
    column_scale = jnp.exp(jax.random.uniform(keys[1], (1, BLK, 1), minval=0.0, maxval=math.log(10.0)))
    values = jnp.clip(jax.random.normal(keys[2], shape), -4.0, 4.0)
    trend = device_trend(DEVS, RT, 3.0)
    return (values * row_scale * column_scale * trend[:, None, None]).astype(jnp.float32)


def draw_tile_values(key, part):
    keys = jax.random.split(jax.random.fold_in(key, 23), 2)
    shape = (DEVS * NT, TILE, TILE)
    row_scale = jnp.exp(jax.random.uniform(keys[0], (DEVS * NT, TILE, 1), minval=0.0, maxval=math.log(10.0)))
    values = jnp.clip(jax.random.normal(keys[1], shape), -4.0, 4.0)
    trend = device_trend(DEVS, NT, 3.0)
    scaled = values * row_scale * trend[:, None, None] / math.sqrt(TPR * TILE)
    return scaled.astype(jnp.float32).astype(jnp.bfloat16)


def draw_tile_count(key, part):
    keys = jax.random.split(jax.random.fold_in(key, 37), 3)
    draws = jax.random.randint(keys[0], (DEVS,), 0, 64)
    counts = NT // 8 + (NT - NT // 8) * draws * draws // 3969
    fullest = jax.random.randint(keys[1], (), 0, DEVS)
    counts = counts.at[fullest].set(NT)
    emptiest = (fullest + 1 + jax.random.randint(keys[2], (), 0, DEVS - 1)) % DEVS
    counts = counts.at[emptiest].set(NT // 8)
    return counts.astype(jnp.int32)


def draw_send_count(key, part):
    keys = jax.random.split(jax.random.fold_in(key, 53), 2)
    counts = jax.random.randint(keys[0], (DEVS, DEVS), CAP // 2, CAP + 1)
    sources = jnp.arange(DEVS, dtype=jnp.int32)
    counts = counts.at[sources, (sources + 1) % DEVS].set(CAP)
    busiest = jax.random.randint(keys[1], (), 0, DEVS)
    counts = counts.at[:, busiest].set(CAP)
    return counts.astype(jnp.int32)


def with_ends(drawn, key, smallest, high):
    shape = drawn.shape
    place = [jax.random.randint(jax.random.fold_in(key, axis), (), 0, shape[axis]) for axis in range(len(shape))]
    drawn = drawn.at[tuple(place)].set(smallest)
    longest = shape.index(max(shape))
    place[longest] = (place[longest] + 1) % shape[longest]
    return drawn.at[tuple(place)].set(high)


def bell_draw(stream_key, dims, spread, reach, kind=jnp.bfloat16):
    drawn = jax.random.normal(stream_key, dims, jnp.float32) * spread
    return jnp.minimum(jnp.maximum(drawn, -reach), reach).astype(kind)


def setup_inputs(seed: int = 0) -> dict:
    seeds = jax.random.split(jax.random.key(seed), 9)
    start_block = draw_start_block(jax.random.fold_in(seeds[8], 71), 0)
    tile_values = draw_tile_values(jax.random.fold_in(seeds[8], 71), 0)
    tile_rows = with_ends(jax.random.randint(seeds[2], (DEVS * NT,), 0, RT), jax.random.fold_in(seeds[2], 1), 0, RT - 1).astype(jnp.int32)
    tile_cols = with_ends(jax.random.randint(seeds[3], (DEVS * NT,), 0, SRC_TILES), jax.random.fold_in(seeds[3], 1), 0, SRC_TILES - 1).astype(jnp.int32)
    tile_count = draw_tile_count(jax.random.fold_in(seeds[8], 71), 0)
    send_rows = with_ends(jax.random.randint(seeds[5], (DEVS, DEVS, CAP), 0, ROWS_DEV), jax.random.fold_in(seeds[5], 1), 0, ROWS_DEV - 1).astype(jnp.int32)
    send_count = draw_send_count(jax.random.fold_in(seeds[8], 71), 0)
    rotation = bell_draw(seeds[7], (BASIS, BLK), BASIS ** -0.5, 0.4375, jnp.float32)
    return {"start_block": start_block, "tile_values": tile_values, "tile_rows": tile_rows, "tile_cols": tile_cols, "tile_count": tile_count, "send_rows": send_rows, "send_count": send_count, "rotation": rotation}


HIGHEST_PRECISION = lax.Precision.HIGHEST

def inner_mean(left_block, right_block):
    return jnp.einsum('tai,tbi->ab', left_block, right_block, precision=HIGHEST_PRECISION) / NODES

def normalize(product_block):
    factor = jnp.linalg.cholesky(inner_mean(product_block, product_block))
    inverse = lax.linalg.triangular_solve(factor, jnp.eye(BLK, dtype=jnp.float32), left_side=True, lower=True)
    return jnp.einsum('ab,tbi->tai', inverse, product_block, precision=HIGHEST_PRECISION)

def apply_graph(current, tile_values, tile_rows, tile_cols, tile_count, send_rows, send_count):
    rounded = current.astype(jnp.bfloat16)
    node_rows = rounded.transpose(0, 2, 1).reshape(NODES, BLK)
    slot_index = jnp.arange(CAP, dtype=jnp.int32)
    offsets = jnp.arange(DEVS, dtype=jnp.int32) * ROWS_DEV

    def one_partition(device_index):
        wanted = lax.dynamic_index_in_dim(send_rows, device_index, 1, keepdims=False) + offsets[:, None]
        received = node_rows[wanted.reshape(-1)].reshape(DEVS, CAP, BLK)
        counts = lax.dynamic_index_in_dim(send_count, device_index, 1, keepdims=False)
        kept_slots = slot_index[None, :] < counts[:, None]
        received = jnp.where(kept_slots[:, :, None], received, jnp.zeros_like(received))
        halo_block = received.reshape(HALO_TILES, TILE, BLK).transpose(0, 2, 1)
        own_block = lax.dynamic_slice_in_dim(rounded, (device_index * RT).astype(jnp.int32), RT, 0)
        source = jnp.concatenate([own_block, halo_block], 0)
        first_slot = (device_index * NT).astype(jnp.int32)
        values = lax.dynamic_slice_in_dim(tile_values, first_slot, NT, 0)
        row_index = lax.dynamic_slice_in_dim(tile_rows, first_slot, NT, 0)
        col_index = lax.dynamic_slice_in_dim(tile_cols, first_slot, NT, 0)
        picked = source[col_index]
        products = jnp.einsum('kbj,kij->kbi', picked.astype(jnp.float32), values.astype(jnp.float32), precision=HIGHEST_PRECISION)
        live_slots = jnp.arange(NT, dtype=jnp.int32) < tile_count[device_index]
        products = jnp.where(live_slots[:, None, None], products, jnp.zeros_like(products))
        return jax.ops.segment_sum(products, row_index, num_segments=RT)
    result = lax.map(one_partition, jnp.arange(DEVS, dtype=jnp.int32))
    return result.reshape(ROW_TILES, BLK, TILE)

def reference(start_block, tile_values, tile_rows, tile_cols, tile_count, send_rows, send_count, rotation):
    vectors = [normalize(start_block)]
    for krylov_step in range(2):
        product_block = apply_graph(vectors[-1], tile_values, tile_rows, tile_cols, tile_count, send_rows, send_count)
        stacked = jnp.concatenate(vectors, 1)
        coefficients = inner_mean(stacked, product_block)
        residual_block = product_block - jnp.einsum('ab,tai->tbi', coefficients, stacked, precision=HIGHEST_PRECISION)
        vectors.append(normalize(residual_block))
    all_vectors = jnp.concatenate(vectors, 1)
    return jnp.einsum('jb,tji->tbi', rotation, all_vectors, precision=HIGHEST_PRECISION)
```

```python
import jax
import jax.numpy as jnp
from jax import lax
from jax.sharding import PartitionSpec as P

from jax.experimental import pallas as pl
from jax.experimental.pallas import tpu as pltpu

MESH = pl.DeviceIdType.MESH
HIGHEST_PRECISION = lax.Precision.HIGHEST


def ar_kernel(x_ref,o_ref,pbuf,xybuf,zbuf,fin,ss,rs):
    row=lax.axis_index("row"); col=lax.axis_index("col")
    core=lax.rem(row,2); z=row//2
    prow=row+1-2*core
    H=x_ref.shape[0]//2
    bar=pltpu.get_barrier_semaphore()
    pl.semaphore_signal(bar,inc=1,device_id=(prow,col),device_id_type=MESH)
    def sg(i,c):
        pl.semaphore_signal(bar,inc=1,device_id=(row,lax.rem(col+i,16)),device_id_type=MESH); return c
    lax.fori_loop(1,16,sg,0)
    def sg2(i,c):
        pl.semaphore_signal(bar,inc=1,device_id=(lax.rem(row+2*i,16),col),device_id_type=MESH); return c
    lax.fori_loop(1,8,sg2,0)
    pl.semaphore_wait(bar,23)
    mine=pl.ds(pl.multiple_of(core*H,H),H); other=pl.ds(pl.multiple_of((1-core)*H,H),H)
    cp=pltpu.make_async_remote_copy(x_ref.at[other],pbuf,ss.at[0],rs.at[0],device_id=(prow,col),device_id_type=MESH)
    cp.start(); cp.wait()
    xybuf[col]=x_ref[mine,:]+pbuf[...]
    def s1(i,c):
        pltpu.make_async_remote_copy(xybuf.at[col],xybuf.at[col],ss.at[1],rs.at[1],device_id=(row,lax.rem(col+i,16)),device_id_type=MESH).start(); return c
    lax.fori_loop(1,16,s1,0)
    w=pltpu.make_async_remote_copy(xybuf.at[pl.ds(0,15)],xybuf.at[pl.ds(0,15)],ss.at[1],rs.at[1],device_id=(prow,col),device_id_type=MESH)
    w.wait_recv(); w.wait_send()
    zbuf[z]=jnp.sum(xybuf[...],axis=0)
    def s2(i,c):
        pltpu.make_async_remote_copy(zbuf.at[z],zbuf.at[z],ss.at[2],rs.at[2],device_id=(lax.rem(row+2*i,16),col),device_id_type=MESH).start(); return c
    lax.fori_loop(1,8,s2,0)
    w=pltpu.make_async_remote_copy(zbuf.at[pl.ds(0,7)],zbuf.at[pl.ds(0,7)],ss.at[2],rs.at[2],device_id=(prow,col),device_id_type=MESH)
    w.wait_recv(); w.wait_send()
    fin[mine,:]=jnp.sum(zbuf[...],axis=0)
    cp=pltpu.make_async_remote_copy(fin.at[mine],fin.at[mine],ss.at[3],rs.at[3],device_id=(prow,col),device_id_type=MESH)
    cp.start(); cp.wait()
    o_ref[...]=fin[...]

def allreduce(x,cid):
    R=x.shape[0];H=R//2
    return pl.pallas_call(ar_kernel,out_shape=jax.ShapeDtypeStruct(x.shape,jnp.float32),
      in_specs=[pl.BlockSpec(memory_space=pltpu.VMEM)],out_specs=pl.BlockSpec(memory_space=pltpu.VMEM),
      scratch_shapes=[pltpu.VMEM((H,128),jnp.float32),pltpu.VMEM((16,H,128),jnp.float32),pltpu.VMEM((8,H,128),jnp.float32),pltpu.VMEM((R,128),jnp.float32),
        pltpu.SemaphoreType.DMA((4,)),pltpu.SemaphoreType.DMA((4,))],
      compiler_params=pltpu.CompilerParams(collective_id=cid,has_side_effects=True))(x)

def ex_kernel(s_ref,o_ref,ss,rs,ls):
    row=lax.axis_index("row"); col=lax.axis_index("col")
    me=row*16+col
    lc=pltpu.make_async_copy(s_ref.at[me],o_ref.at[me],ls); lc.start()
    def go(i,c):
        dr=lax.rem(i,16); dc=i//16
        r2=lax.rem(row+dr,16); c2=lax.rem(col+dc,16)
        pltpu.make_async_remote_copy(s_ref.at[r2*16+c2],o_ref.at[me],ss,rs,device_id=(r2,c2),device_id_type=MESH).start()
        return c
    lax.fori_loop(1,256,go,0)
    w=pltpu.make_async_remote_copy(s_ref.at[pl.ds(0,255)],o_ref.at[pl.ds(0,255)],ss,rs,device_id=(row,lax.rem(col+1,16)),device_id_type=MESH)
    w.wait_recv(); w.wait_send(); lc.wait()
def exchange(x):
    return pl.pallas_call(ex_kernel,out_shape=jax.ShapeDtypeStruct(x.shape,x.dtype),
      in_specs=[pl.BlockSpec(memory_space=pltpu.VMEM)],out_specs=pl.BlockSpec(memory_space=pltpu.VMEM),
      scratch_shapes=[pltpu.SemaphoreType.DMA]*3,
      compiler_params=pltpu.CompilerParams(has_side_effects=True))(x)


def total(x):
    return allreduce(x.reshape(x.shape[0]//2,128),x.shape[0]//64).reshape(x.shape)


def local_inner(left_block, right_block):
    return jnp.einsum("tai,tbi->ab", left_block, right_block, precision=HIGHEST_PRECISION)


def unit_columns(product_block, gram_matrix):
    factor = jnp.linalg.cholesky(gram_matrix)
    inverse = lax.linalg.triangular_solve(
        factor, jnp.eye(factor.shape[0], dtype=jnp.float32), left_side=True, lower=True
    )
    return jnp.einsum("ab,tbi->tai", inverse, product_block, precision=HIGHEST_PRECISION)


def apply_graph(current, tile_values, tile_rows, tile_cols, tile_count, send_rows, send_count):
    row_tiles, block_width, tile_size = current.shape
    rounded = current.astype(jnp.bfloat16)
    node_rows = rounded.transpose(0, 2, 1).reshape(row_tiles * tile_size, block_width)
    targets = send_rows[0]
    partitions, capacity = targets.shape
    chosen = node_rows[targets.reshape(-1)].reshape(partitions, capacity, block_width)
    kept_slots = jnp.arange(capacity, dtype=jnp.int32)[None, :] < send_count[0][:, None]
    chosen = jnp.where(kept_slots[:, :, None], chosen, jnp.zeros_like(chosen))
    incoming = exchange(chosen.reshape(partitions, capacity * block_width // 128, 128))
    halo_count = partitions * capacity // tile_size
    halo_block = incoming.reshape(halo_count, tile_size, block_width).transpose(0, 2, 1)
    source = jnp.concatenate([rounded, halo_block], 0)
    picked = source[tile_cols]
    products = jnp.einsum("kbj,kij->kbi", picked, tile_values, preferred_element_type=jnp.float32)
    slot_total = tile_cols.shape[0]
    live_slots = jnp.arange(slot_total, dtype=jnp.int32) < tile_count[0]
    owner_table = (
        tile_rows[None, :] == jnp.arange(row_tiles, dtype=jnp.int32)[:, None]
    ) & live_slots[None, :]
    return jnp.einsum(
        "rk,kbi->rbi", owner_table.astype(jnp.float32), products, precision=HIGHEST_PRECISION
    )


def body(
    start_block, tile_values, tile_rows, tile_cols, tile_count, send_rows, send_count, rotation
):
    node_total = (
        start_block.shape[0] * start_block.shape[2] * lax.axis_size("row") * lax.axis_size("col")
    )
    start_sum = total(local_inner(start_block, start_block))
    vectors = [unit_columns(start_block, start_sum / node_total)]
    for krylov_step in range(2):
        product_block = apply_graph(
            vectors[-1], tile_values, tile_rows, tile_cols, tile_count, send_rows, send_count
        )
        stacked = jnp.concatenate(vectors, 1)
        coefficients = total(local_inner(stacked, product_block)) / node_total
        residual_block = product_block - jnp.einsum(
            "ab,tai->tbi", coefficients, stacked, precision=HIGHEST_PRECISION
        )
        gram_matrix = (
            total(local_inner(residual_block, residual_block)) / node_total
        )
        vectors.append(unit_columns(residual_block, gram_matrix))
    all_vectors = jnp.concatenate(vectors, 1)
    return jnp.einsum("jb,tji->tbi", rotation, all_vectors, precision=HIGHEST_PRECISION)


def solution(mesh):
    return jax.shard_map(
        body,
        mesh=mesh,
        in_specs=(
            P(("row", "col"), None, None),
            P(("row", "col"), None, None),
            P(("row", "col")),
            P(("row", "col")),
            P(("row", "col")),
            P(("row", "col"), None, None),
            P(("row", "col"), None),
            P(),
        ),
        out_specs=P(("row", "col"), None, None),
        check_vma=False,
    )
```

```python
import functools

import jax
import jax.numpy as jnp
from jax import lax
from jax.experimental import pallas as pl
from jax.experimental.pallas import tpu as pltpu
from jax.sharding import PartitionSpec as P

MESH = pl.DeviceIdType.MESH
HIGHEST = lax.Precision.HIGHEST
F32 = jnp.float32
BF16 = jnp.bfloat16
RT = 16
BLK = 64
TILE = 128
DEVS = 256
NODES = 524288
CHUNK = 16
VMEM = pl.BlockSpec(memory_space=pltpu.VMEM)
SMEM = pl.BlockSpec(memory_space=pltpu.SMEM)


def ar_kernel(x_ref, o_ref, pbuf, xybuf, zbuf, fin, ss, rs):
    row = lax.axis_index("row")
    col = lax.axis_index("col")
    core = lax.rem(row, 2)
    z = row // 2
    prow = row + 1 - 2 * core
    half = x_ref.shape[0] // 2
    bar = pltpu.get_barrier_semaphore()
    pl.semaphore_signal(bar, inc=1, device_id=(prow, col), device_id_type=MESH)

    def greet_xy(i, c):
        pl.semaphore_signal(bar, inc=1, device_id=(row, lax.rem(col + i, 16)), device_id_type=MESH)
        return c

    lax.fori_loop(1, 16, greet_xy, 0)

    def greet_z(i, c):
        pl.semaphore_signal(bar, inc=1, device_id=(lax.rem(row + 2 * i, 16), col), device_id_type=MESH)
        return c

    lax.fori_loop(1, 8, greet_z, 0)
    pl.semaphore_wait(bar, 23)
    mine = pl.ds(pl.multiple_of(core * half, half), half)
    other = pl.ds(pl.multiple_of((1 - core) * half, half), half)
    cp = pltpu.make_async_remote_copy(
        x_ref.at[other], pbuf, ss.at[0], rs.at[0], device_id=(prow, col), device_id_type=MESH
    )
    cp.start()
    cp.wait()
    xybuf[col] = x_ref[mine, :] + pbuf[...]

    def send_xy(i, c):
        pltpu.make_async_remote_copy(
            xybuf.at[col], xybuf.at[col], ss.at[1], rs.at[1],
            device_id=(row, lax.rem(col + i, 16)), device_id_type=MESH,
        ).start()
        return c

    lax.fori_loop(1, 16, send_xy, 0)
    w = pltpu.make_async_remote_copy(
        xybuf.at[pl.ds(0, 15)], xybuf.at[pl.ds(0, 15)], ss.at[1], rs.at[1],
        device_id=(prow, col), device_id_type=MESH,
    )
    w.wait_recv()
    w.wait_send()
    zbuf[z] = jnp.sum(xybuf[...], axis=0)

    def send_z(i, c):
        pltpu.make_async_remote_copy(
            zbuf.at[z], zbuf.at[z], ss.at[2], rs.at[2],
            device_id=(lax.rem(row + 2 * i, 16), col), device_id_type=MESH,
        ).start()
        return c

    lax.fori_loop(1, 8, send_z, 0)
    w = pltpu.make_async_remote_copy(
        zbuf.at[pl.ds(0, 7)], zbuf.at[pl.ds(0, 7)], ss.at[2], rs.at[2],
        device_id=(prow, col), device_id_type=MESH,
    )
    w.wait_recv()
    w.wait_send()
    fin[mine, :] = jnp.sum(zbuf[...], axis=0)
    cp = pltpu.make_async_remote_copy(
        fin.at[mine], fin.at[mine], ss.at[3], rs.at[3], device_id=(prow, col), device_id_type=MESH
    )
    cp.start()
    cp.wait()
    o_ref[...] = fin[...]


def allreduce(x):
    rows = x.shape[0]
    half = rows // 2
    return pl.pallas_call(
        ar_kernel,
        out_shape=jax.ShapeDtypeStruct(x.shape, F32),
        in_specs=[VMEM],
        out_specs=VMEM,
        scratch_shapes=[
            pltpu.VMEM((half, 128), F32),
            pltpu.VMEM((16, half, 128), F32),
            pltpu.VMEM((8, half, 128), F32),
            pltpu.VMEM((rows, 128), F32),
            pltpu.SemaphoreType.DMA((4,)),
            pltpu.SemaphoreType.DMA((4,)),
        ],
        compiler_params=pltpu.CompilerParams(collective_id=rows // 32, has_side_effects=True),
    )(x)


def ex_kernel(s_ref, o_ref, ss, rs, ls):
    row = lax.axis_index("row")
    col = lax.axis_index("col")
    me = row * 16 + col
    lc = pltpu.make_async_copy(s_ref.at[me], o_ref.at[me], ls)
    lc.start()

    def go(i, c):
        r2 = lax.rem(row + lax.rem(i, 16), 16)
        c2 = lax.rem(col + i // 16, 16)
        pltpu.make_async_remote_copy(
            s_ref.at[r2 * 16 + c2], o_ref.at[me], ss, rs, device_id=(r2, c2), device_id_type=MESH
        ).start()
        return c

    lax.fori_loop(1, 256, go, 0)
    w = pltpu.make_async_remote_copy(
        s_ref.at[pl.ds(0, 255)], o_ref.at[pl.ds(0, 255)], ss, rs,
        device_id=(row, lax.rem(col + 1, 16)), device_id_type=MESH,
    )
    w.wait_recv()
    w.wait_send()
    lc.wait()


def exchange(x):
    return pl.pallas_call(
        ex_kernel,
        out_shape=jax.ShapeDtypeStruct(x.shape, x.dtype),
        in_specs=[VMEM],
        out_specs=VMEM,
        scratch_shapes=[pltpu.SemaphoreType.DMA] * 3,
        compiler_params=pltpu.CompilerParams(has_side_effects=True),
    )(x)


def nt(a, b):
    return lax.dot_general(a, b, (((1,), (1,)), ((), ())), precision=HIGHEST, preferred_element_type=F32)


def nn(a, b):
    return lax.dot_general(a, b, (((1,), (0,)), ((), ())), precision=HIGHEST, preferred_element_type=F32)


def wide(ref):
    return jnp.concatenate([ref[t] for t in range(RT)], axis=1)


def put_wide(ref, x):
    for t in range(RT):
        ref[t] = x[:, t * TILE:(t + 1) * TILE].astype(ref.dtype)


def fold(g):
    return jnp.concatenate([g[:32], g[32:]], axis=1)


def unfold(p):
    return jnp.concatenate([p[:, :64], p[:, 64:]], axis=0)


def inverse_factor(g):
    lane = lax.broadcasted_iota(jnp.int32, (8, 128), 1)
    sub = lax.broadcasted_iota(jnp.int32, (8, 128), 0)
    wide_g = jnp.concatenate([g, jnp.zeros((64, 64), F32)], axis=1)
    blocks = [
        jnp.where(lane == sub + (64 + 8 * b), 1.0, wide_g[8 * b:8 * b + 8]) for b in range(8)
    ]
    for j in range(64):
        jb, jr = divmod(j, 8)
        pivot_row = blocks[jb][jr:jr + 1, :]
        scaled = pivot_row / pivot_row[:, j:j + 1]
        for b in range(jb, 8):
            c = blocks[b][:, j:j + 1]
            if b == jb:
                c = jnp.where(sub[:, :1] > jr, c, 0.0)
            blocks[b] = blocks[b] - c * scaled
    out = []
    for b in range(8):
        d = jnp.sum(jnp.where(lane == sub + 8 * b, blocks[b], 0.0), axis=1, keepdims=True)
        out.append(blocks[b][:, 64:] / jnp.sqrt(d))
    return jnp.concatenate(out, axis=0)


def swap_groups(parts):
    lane = lax.broadcasted_iota(jnp.int32, (16, 128), 1)
    low = lane < 64
    even = lax.rem(lane, 64) < 32
    first = {}
    for g in range(2):
        a, b = parts[g], parts[g + 2]
        first[0, g] = jnp.where(low, a, pltpu.roll(b, 64, 1))
        first[1, g] = jnp.where(low, pltpu.roll(a, 64, 1), b)
    out = []
    for h in range(2):
        a, b = first[h, 0], first[h, 1]
        out.append(jnp.where(even, a, pltpu.roll(b, 32, 1)))
        out.append(jnp.where(even, pltpu.roll(a, 96, 1), b))
    return out


def gram_kernel(x_ref, o_ref):
    x = wide(x_ref)
    o_ref[...] = fold(nt(x, x))


def ortho_kernel(z_ref, g_ref, l_ref, t_ref, q_ref, p_ref, s_ref, lhs):
    m = inverse_factor(unfold(g_ref[...]) * (1.0 / NODES))
    put_wide(q_ref, nn(m, wide(z_ref)))
    for t in range(RT):
        p_ref[t] = q_ref[t].astype(BF16)
        lhs[64 * (t // 2):64 * (t // 2) + 64, 128 * (t % 2):128 * (t % 2) + 128] = q_ref[t].astype(BF16)
    node = lax.broadcasted_iota(jnp.int32, (256, 256), 0)

    def chunk(c, carry):
        lsel = jnp.concatenate([l_ref[pl.ds(2 * c, 1), :], l_ref[pl.ds(2 * c + 1, 1), :]], axis=1)
        tsel = jnp.concatenate([t_ref[pl.ds(2 * c, 1), :], t_ref[pl.ds(2 * c + 1, 1), :]], axis=1)
        hot = jnp.where(node == lsel, 1.0, 0.0).astype(BF16)
        r = jnp.dot(lhs[...], hot, preferred_element_type=F32)
        acc = jnp.zeros((64, 256), F32)
        for t in range(8):
            acc = acc + jnp.where(tsel == t, r[64 * t:64 * t + 64], 0.0)
        for h in range(2):
            msgs = swap_groups([acc[16 * g:16 * g + 16, 128 * h:128 * h + 128] for g in range(4)])
            for q in range(4):
                s_ref[8 * c + 4 * h + q] = msgs[q].astype(BF16)
        return carry

    lax.fori_loop(0, 32, chunk, 0)


def apply_kernel(nb, *refs):
    rows, cols, count, values, p_ref, h_ref = refs[:6]
    basis = refs[6:6 + nb]
    y_ref, c_ref, src, acc, buf, sem = refs[6 + nb:]
    n = count[0]
    nchunk = (n + CHUNK - 1) // CHUNK

    def fetch(c):
        slot = lax.rem(c, 3)
        return pltpu.make_async_copy(values.at[pl.ds(c * CHUNK, CHUNK)], buf.at[slot], sem.at[slot])

    fetch(0).start()

    @pl.when(nchunk > 1)
    def _():
        fetch(1).start()

    acc[...] = jnp.zeros_like(acc)
    src[0:RT] = p_ref[...]

    def unpack(h, c):
        parts = swap_groups([h_ref[4 * h + q].astype(F32) for q in range(4)])
        for g in range(4):
            src[RT + h, 16 * g:16 * g + 16, :] = parts[g].astype(BF16)
        return c

    lax.fori_loop(0, 64, unpack, 0)

    def step(c, carry):
        @pl.when(c + 2 < nchunk)
        def _():
            fetch(c + 2).start()

        fetch(c).wait()
        slot = lax.rem(c, 3)
        for u in range(CHUNK):
            k = c * CHUNK + u
            r = jnp.where(k < n, rows[k], RT)
            acc[r] += lax.dot_general(
                src[cols[k]], buf[slot, u], (((1,), (1,)), ((), ())), preferred_element_type=F32
            )
        return carry

    lax.fori_loop(0, nchunk, step, 0)
    y_ref[...] = acc[0:RT]
    y = wide(acc)
    c_ref[...] = jnp.concatenate([fold(nt(y, wide(b))) for b in basis], axis=0)


def project_kernel(nb, *refs):
    y_ref, c_ref = refs[:2]
    basis = refs[2:2 + nb]
    z_ref, g_ref = refs[2 + nb:]
    z = wide(y_ref)
    for i, b in enumerate(basis):
        z = z - nn(unfold(c_ref[32 * i:32 * i + 32]) * (1.0 / NODES), wide(b))
    put_wide(z_ref, z)
    g_ref[...] = fold(nt(z, z))


def final_kernel(z_ref, g_ref, rot_ref, q0_ref, q1_ref, o_ref):
    m = inverse_factor(unfold(g_ref[...]) * (1.0 / NODES))
    rot = rot_ref[...]
    tail = nn(rot[:, 128:192], m)
    o = nn(rot[:, 0:64], wide(q0_ref)) + nn(rot[:, 64:128], wide(q1_ref)) + nn(tail, wide(z_ref))
    put_wide(o_ref, o)


def block(dtype):
    return jax.ShapeDtypeStruct((RT, BLK, TILE), dtype)


def gram(x):
    return pl.pallas_call(
        gram_kernel, out_shape=jax.ShapeDtypeStruct((32, 128), F32), in_specs=[VMEM], out_specs=VMEM
    )(x)


def ortho(z, g, lsel, tsel):
    return pl.pallas_call(
        ortho_kernel,
        out_shape=(block(F32), block(BF16), jax.ShapeDtypeStruct((DEVS, 16, 128), BF16)),
        in_specs=[VMEM] * 4,
        out_specs=(VMEM,) * 3,
        scratch_shapes=[pltpu.VMEM((512, 256), BF16)],
    )(z, g, lsel, tsel)


def apply_graph(rows, cols, count, values, p, halo, basis):
    nb = len(basis)
    return pl.pallas_call(
        functools.partial(apply_kernel, nb),
        out_shape=(block(F32), jax.ShapeDtypeStruct((32 * nb, 128), F32)),
        in_specs=[SMEM] * 3 + [pl.BlockSpec(memory_space=pl.ANY)] + [VMEM] * (2 + nb),
        out_specs=(VMEM,) * 2,
        scratch_shapes=[
            pltpu.VMEM((80, BLK, TILE), BF16),
            pltpu.VMEM((RT + 1, BLK, TILE), F32),
            pltpu.VMEM((3, CHUNK, TILE, TILE), BF16),
            pltpu.SemaphoreType.DMA((3,)),
        ],
    )(rows, cols, count, values, p, halo, *basis)


def project(y, c, basis):
    nb = len(basis)
    return pl.pallas_call(
        functools.partial(project_kernel, nb),
        out_shape=(block(F32), jax.ShapeDtypeStruct((32, 128), F32)),
        in_specs=[VMEM] * (2 + nb),
        out_specs=(VMEM,) * 2,
    )(y, c, *basis)


def body(start, values, rows, cols, count, send_rows, send_count, rotation):
    slot = jnp.arange(32, dtype=jnp.int32)
    wanted = send_rows[0]
    lsel = (wanted % 256).reshape(64, 128)
    tsel = jnp.where(slot[None, :] < send_count[0][:, None], wanted // 256, -1).reshape(64, 128)
    g = allreduce(gram(start))
    q, p, out = ortho(start, g, lsel, tsel)
    basis = [q]
    for k in range(2):
        halo = exchange(out)
        y, c = apply_graph(rows, cols, count, values, p, halo, basis)
        z, g = project(y, allreduce(c), basis)
        g = allreduce(g)
        if k == 0:
            q, p, out = ortho(z, g, lsel, tsel)
            basis.append(q)
    return pl.pallas_call(
        final_kernel, out_shape=block(F32), in_specs=[VMEM] * 5, out_specs=VMEM
    )(z, g, rotation.T, basis[0], basis[1])


def solution(mesh):
    spec = P(("row", "col"))
    return jax.shard_map(
        body,
        mesh=mesh,
        in_specs=(spec,) * 7 + (P(),),
        out_specs=spec,
        check_vma=False,
    )
```

```python
import functools

import jax
import jax.numpy as jnp
from jax import lax
from jax.experimental import pallas as pl
from jax.experimental.pallas import tpu as pltpu
from jax.sharding import PartitionSpec as P

MESH = pl.DeviceIdType.MESH
HIGHEST = lax.Precision.HIGHEST
F32 = jnp.float32
BF16 = jnp.bfloat16
RT = 16
BLK = 64
TILE = 128
DEVS = 256
NODES = 524288
CHUNK = 16
VMEM = pl.BlockSpec(memory_space=pltpu.VMEM)
SMEM = pl.BlockSpec(memory_space=pltpu.SMEM)


def place():
    row = lax.axis_index("row")
    col = lax.axis_index("col")
    return row, col, row + 1 - 2 * lax.rem(row, 2)


def greet():
    row, col, prow = place()
    bar = pltpu.get_barrier_semaphore()
    pl.semaphore_signal(bar, inc=1, device_id=(prow, col), device_id_type=MESH)

    def greet_xy(i, c):
        pl.semaphore_signal(bar, inc=1, device_id=(row, lax.rem(col + i, 16)), device_id_type=MESH)
        return c

    lax.fori_loop(1, 16, greet_xy, 0)

    def greet_z(i, c):
        pl.semaphore_signal(bar, inc=1, device_id=(lax.rem(row + 2 * i, 16), col), device_id_type=MESH)
        return c

    lax.fori_loop(1, 8, greet_z, 0)


def greeted():
    pl.semaphore_wait(pltpu.get_barrier_semaphore(), 23)


def sum_scratch(rows):
    half = rows // 2
    return [
        pltpu.VMEM((rows, 128), F32),
        pltpu.VMEM((half, 128), F32),
        pltpu.VMEM((16, half, 128), F32),
        pltpu.VMEM((8, half, 128), F32),
        pltpu.VMEM((rows, 128), F32),
        pltpu.SemaphoreType.DMA((4,)),
        pltpu.SemaphoreType.DMA((4,)),
    ]


def total(scratch):
    xbuf, pbuf, xybuf, zbuf, fin, ss, rs = scratch
    row, col, prow = place()
    core = lax.rem(row, 2)
    z = row // 2
    half = pbuf.shape[0]
    mine = pl.ds(pl.multiple_of(core * half, half), half)
    other = pl.ds(pl.multiple_of((1 - core) * half, half), half)
    cp = pltpu.make_async_remote_copy(
        xbuf.at[other], pbuf, ss.at[0], rs.at[0], device_id=(prow, col), device_id_type=MESH
    )
    cp.start()
    cp.wait()
    xybuf[col] = xbuf[mine, :] + pbuf[...]

    def send_xy(i, c):
        pltpu.make_async_remote_copy(
            xybuf.at[col], xybuf.at[col], ss.at[1], rs.at[1],
            device_id=(row, lax.rem(col + i, 16)), device_id_type=MESH,
        ).start()
        return c

    lax.fori_loop(1, 16, send_xy, 0)
    w = pltpu.make_async_remote_copy(
        xybuf.at[pl.ds(0, 15)], xybuf.at[pl.ds(0, 15)], ss.at[1], rs.at[1],
        device_id=(prow, col), device_id_type=MESH,
    )
    w.wait_recv()
    w.wait_send()
    zbuf[z] = jnp.sum(xybuf[...], axis=0)

    def send_z(i, c):
        pltpu.make_async_remote_copy(
            zbuf.at[z], zbuf.at[z], ss.at[2], rs.at[2],
            device_id=(lax.rem(row + 2 * i, 16), col), device_id_type=MESH,
        ).start()
        return c

    lax.fori_loop(1, 8, send_z, 0)
    w = pltpu.make_async_remote_copy(
        zbuf.at[pl.ds(0, 7)], zbuf.at[pl.ds(0, 7)], ss.at[2], rs.at[2],
        device_id=(prow, col), device_id_type=MESH,
    )
    w.wait_recv()
    w.wait_send()
    fin[mine, :] = jnp.sum(zbuf[...], axis=0)
    cp = pltpu.make_async_remote_copy(
        fin.at[mine], fin.at[mine], ss.at[3], rs.at[3], device_id=(prow, col), device_id_type=MESH
    )
    cp.start()
    cp.wait()
    return fin[...]


def nt(a, b):
    return lax.dot_general(a, b, (((1,), (1,)), ((), ())), precision=HIGHEST, preferred_element_type=F32)


def nn(a, b):
    return lax.dot_general(a, b, (((1,), (0,)), ((), ())), precision=HIGHEST, preferred_element_type=F32)


def wide(ref):
    return jnp.concatenate([ref[t] for t in range(RT)], axis=1)


def put_wide(ref, x):
    for t in range(RT):
        ref[t] = x[:, t * TILE:(t + 1) * TILE].astype(ref.dtype)


def fold(g):
    return jnp.concatenate([g[:32], g[32:]], axis=1)


def unfold(p):
    return jnp.concatenate([p[:, :64], p[:, 64:]], axis=0)


def inverse_factor(g):
    lane = lax.broadcasted_iota(jnp.int32, (8, 128), 1)
    sub = lax.broadcasted_iota(jnp.int32, (8, 128), 0)
    wide_g = jnp.concatenate([g, jnp.zeros((64, 64), F32)], axis=1)
    blocks = [
        jnp.where(lane == sub + (64 + 8 * b), 1.0, wide_g[8 * b:8 * b + 8]) for b in range(8)
    ]
    for j in range(64):
        jb, jr = divmod(j, 8)
        pivot_row = blocks[jb][jr:jr + 1, :]
        scaled = pivot_row / pivot_row[:, j:j + 1]
        for b in range(jb, 8):
            c = blocks[b][:, j:j + 1]
            if b == jb:
                c = jnp.where(sub[:, :1] > jr, c, 0.0)
            blocks[b] = blocks[b] - c * scaled
    out = []
    for b in range(8):
        d = jnp.sum(jnp.where(lane == sub + 8 * b, blocks[b], 0.0), axis=1, keepdims=True)
        out.append(blocks[b][:, 64:] / jnp.sqrt(d))
    return jnp.concatenate(out, axis=0)


def swap_groups(parts):
    lane = lax.broadcasted_iota(jnp.int32, (16, 128), 1)
    low = lane < 64
    even = lax.rem(lane, 64) < 32
    first = {}
    for g in range(2):
        a, b = parts[g], parts[g + 2]
        first[0, g] = jnp.where(low, a, pltpu.roll(b, 64, 1))
        first[1, g] = jnp.where(low, pltpu.roll(a, 64, 1), b)
    out = []
    for h in range(2):
        a, b = first[h, 0], first[h, 1]
        out.append(jnp.where(even, a, pltpu.roll(b, 32, 1)))
        out.append(jnp.where(even, pltpu.roll(a, 96, 1), b))
    return out


def send_halo(q_ref, l_ref, t_ref, h_ref, scratch):
    lhs, out, ss, rs, ls = scratch
    row, col, prow = place()
    me = row * 16 + col
    for t in range(RT):
        lhs[64 * (t // 2):64 * (t // 2) + 64, 128 * (t % 2):128 * (t % 2) + 128] = q_ref[t].astype(BF16)
    node = lax.broadcasted_iota(jnp.int32, (256, 256), 0)

    def target(i):
        return lax.rem(row + 8 + 5 * (i // 2), 16), lax.rem(i, 2) * 8

    def send(i):
        r2, c2 = target(i)
        for u in range(8):
            there = r2 * 16 + c2 + u

            @pl.when(there != me)
            def _():
                pltpu.make_async_remote_copy(
                    out.at[there], h_ref.at[me], ss, rs, device_id=(r2, c2 + u), device_id_type=MESH
                ).start()

    def chunk(i, carry):
        r2, c2 = target(i)
        c = 2 * r2 + c2 // 8
        lsel = jnp.concatenate([l_ref[pl.ds(2 * c, 1), :], l_ref[pl.ds(2 * c + 1, 1), :]], axis=1)
        tsel = jnp.concatenate([t_ref[pl.ds(2 * c, 1), :], t_ref[pl.ds(2 * c + 1, 1), :]], axis=1)
        hot = jnp.where(node == lsel, 1.0, 0.0).astype(BF16)
        r = jnp.dot(lhs[...], hot, preferred_element_type=F32)
        acc = jnp.zeros((64, 256), F32)
        for t in range(8):
            acc = acc + jnp.where(tsel == t, r[64 * t:64 * t + 64], 0.0)
        for h in range(2):
            msgs = swap_groups([acc[16 * g:16 * g + 16, 128 * h:128 * h + 128] for g in range(4)])
            for q in range(4):
                out[8 * c + 4 * h + q] = msgs[q].astype(BF16)

        @pl.when(i > 0)
        def _():
            send(i - 1)

        return carry

    lax.fori_loop(0, 32, chunk, 0)
    send(31)
    own = pltpu.make_async_copy(out.at[me], h_ref.at[me], ls)
    own.start()
    w = pltpu.make_async_remote_copy(
        out.at[pl.ds(0, 255)], h_ref.at[pl.ds(0, 255)], ss, rs,
        device_id=(prow, col), device_id_type=MESH,
    )
    w.wait_recv()
    w.wait_send()
    own.wait()


def halo_scratch():
    return [
        pltpu.VMEM((512, 256), BF16),
        pltpu.VMEM((DEVS, 16, 128), BF16),
        pltpu.SemaphoreType.DMA,
        pltpu.SemaphoreType.DMA,
        pltpu.SemaphoreType.DMA,
    ]


def normalize(z, total_gram, q_ref, p_ref):
    m = inverse_factor(unfold(total_gram) * (1.0 / NODES))
    put_wide(q_ref, nn(m, z))
    p_ref[...] = q_ref[...].astype(BF16)


def first_kernel(x_ref, l_ref, t_ref, q_ref, p_ref, h_ref, *scratch):
    greet()
    x = wide(x_ref)
    scratch[0][...] = fold(nt(x, x))
    greeted()
    g = total(scratch[:7])
    normalize(wide(x_ref), g, q_ref, p_ref)
    send_halo(q_ref, l_ref, t_ref, h_ref, scratch[7:])


def residual(nb, y_ref, basis, c, z_ref):
    z = wide(y_ref)
    for i, b in enumerate(basis):
        z = z - nn(unfold(c[32 * i:32 * i + 32]) * (1.0 / NODES), wide(b))
    put_wide(z_ref, z)
    return fold(nt(z, z))


def next_kernel(y_ref, c_ref, q0_ref, l_ref, t_ref, q_ref, p_ref, h_ref, z_ref, *scratch):
    greet()
    scratch[0][...] = c_ref[...]
    greeted()
    c = total(scratch[:7])
    scratch[7][...] = residual(1, y_ref, [q0_ref], c, z_ref)
    g = total(scratch[7:14])
    normalize(wide(z_ref), g, q_ref, p_ref)
    send_halo(q_ref, l_ref, t_ref, h_ref, scratch[14:])


def last_kernel(y_ref, c_ref, q0_ref, q1_ref, rot_ref, o_ref, z_ref, *scratch):
    greet()
    scratch[0][...] = c_ref[...]
    rot = rot_ref[...]
    greeted()
    c = total(scratch[:7])
    scratch[7][...] = residual(2, y_ref, [q0_ref, q1_ref], c, z_ref)
    g = total(scratch[7:14])
    m = inverse_factor(unfold(g) * (1.0 / NODES))
    tail = nn(rot[:, 128:192], m)
    o = nn(rot[:, 0:64], wide(q0_ref)) + nn(rot[:, 64:128], wide(q1_ref)) + nn(tail, wide(z_ref))
    put_wide(o_ref, o)


def apply_kernel(nb, *refs):
    rows, cols, count, values, p_ref, h_ref = refs[:6]
    basis = refs[6:6 + nb]
    y_ref, c_ref, src, acc, buf, sem = refs[6 + nb:]
    n = count[0]
    nchunk = (n + CHUNK - 1) // CHUNK

    def fetch(c):
        slot = lax.rem(c, 3)
        return pltpu.make_async_copy(values.at[pl.ds(c * CHUNK, CHUNK)], buf.at[slot], sem.at[slot])

    fetch(0).start()

    @pl.when(nchunk > 1)
    def _():
        fetch(1).start()

    acc[...] = jnp.zeros_like(acc)
    src[0:RT] = p_ref[...]

    def unpack(h, c):
        parts = swap_groups([h_ref[4 * h + q].astype(F32) for q in range(4)])
        for g in range(4):
            src[RT + h, 16 * g:16 * g + 16, :] = parts[g].astype(BF16)
        return c

    lax.fori_loop(0, 64, unpack, 0)

    def step(c, carry):
        @pl.when(c + 2 < nchunk)
        def _():
            fetch(c + 2).start()

        fetch(c).wait()
        slot = lax.rem(c, 3)
        for u in range(CHUNK):
            k = c * CHUNK + u
            r = jnp.where(k < n, rows[k], RT)
            acc[r] += lax.dot_general(
                src[cols[k]], buf[slot, u], (((1,), (1,)), ((), ())), preferred_element_type=F32
            )
        return carry

    lax.fori_loop(0, nchunk, step, 0)
    y_ref[...] = acc[0:RT]
    y = wide(acc)
    c_ref[...] = jnp.concatenate([fold(nt(y, wide(b))) for b in basis], axis=0)


def block(dtype):
    return jax.ShapeDtypeStruct((RT, BLK, TILE), dtype)


def remote(kernel, cid, outs, scratch, *operands):
    return pl.pallas_call(
        kernel,
        out_shape=outs,
        in_specs=[VMEM] * len(operands),
        out_specs=(VMEM,) * len(outs),
        scratch_shapes=scratch,
        compiler_params=pltpu.CompilerParams(collective_id=cid, has_side_effects=True),
    )(*operands)


def apply_graph(rows, cols, count, values, p, halo, basis):
    nb = len(basis)
    return pl.pallas_call(
        functools.partial(apply_kernel, nb),
        out_shape=(block(F32), jax.ShapeDtypeStruct((32 * nb, 128), F32)),
        in_specs=[SMEM] * 3 + [pl.BlockSpec(memory_space=pl.ANY)] + [VMEM] * (2 + nb),
        out_specs=(VMEM,) * 2,
        scratch_shapes=[
            pltpu.VMEM((80, BLK, TILE), BF16),
            pltpu.VMEM((RT + 1, BLK, TILE), F32),
            pltpu.VMEM((3, CHUNK, TILE, TILE), BF16),
            pltpu.SemaphoreType.DMA((3,)),
        ],
    )(rows, cols, count, values, p, halo, *basis)


def body(start, values, rows, cols, count, send_rows, send_count, rotation):
    slot = jnp.arange(32, dtype=jnp.int32)
    wanted = send_rows[0]
    lsel = (wanted % 256).reshape(64, 128)
    tsel = jnp.where(slot[None, :] < send_count[0][:, None], wanted // 256, -1).reshape(64, 128)
    state = (block(F32), block(BF16), jax.ShapeDtypeStruct((DEVS, 16, 128), BF16))
    held = [pltpu.VMEM((RT, BLK, TILE), F32)]
    q0, p, halo = remote(first_kernel, 1, state, sum_scratch(32) + halo_scratch(), start, lsel, tsel)
    y, c = apply_graph(rows, cols, count, values, p, halo, [q0])
    q1, p, halo = remote(
        next_kernel, 2, state, held + sum_scratch(32) + sum_scratch(32) + halo_scratch(), y, c, q0, lsel, tsel
    )
    y, c = apply_graph(rows, cols, count, values, p, halo, [q0, q1])
    return remote(
        last_kernel, 3, (block(F32),), held + sum_scratch(64) + sum_scratch(32), y, c, q0, q1, rotation.T
    )[0]


def solution(mesh):
    spec = P(("row", "col"))
    return jax.shard_map(
        body,
        mesh=mesh,
        in_specs=(spec,) * 7 + (P(),),
        out_specs=spec,
        check_vma=False,
    )
```

```python
import functools

import jax
import jax.numpy as jnp
from jax import lax
from jax.experimental import pallas as pl
from jax.experimental.pallas import tpu as pltpu
from jax.sharding import PartitionSpec as P

MESH = pl.DeviceIdType.MESH
HIGHEST = lax.Precision.HIGHEST
F32 = jnp.float32
BF16 = jnp.bfloat16
RT = 16
BLK = 64
TILE = 128
DEVS = 256
NODES = 524288
CHUNK = 16
VMEM = pl.BlockSpec(memory_space=pltpu.VMEM)
SMEM = pl.BlockSpec(memory_space=pltpu.SMEM)


def place():
    row = lax.axis_index("row")
    col = lax.axis_index("col")
    return row, col, row + 1 - 2 * lax.rem(row, 2)


def greet():
    row, col, prow = place()
    bar = pltpu.get_barrier_semaphore()
    pl.semaphore_signal(bar, inc=1, device_id=(prow, col), device_id_type=MESH)

    def greet_xy(i, c):
        pl.semaphore_signal(bar, inc=1, device_id=(row, lax.rem(col + i, 16)), device_id_type=MESH)
        return c

    lax.fori_loop(1, 16, greet_xy, 0)

    def greet_z(i, c):
        pl.semaphore_signal(bar, inc=1, device_id=(lax.rem(row + 2 * i, 16), col), device_id_type=MESH)
        return c

    lax.fori_loop(1, 8, greet_z, 0)


def greeted():
    pl.semaphore_wait(pltpu.get_barrier_semaphore(), 23)


def sum_scratch(rows):
    half = rows // 2
    return [
        pltpu.VMEM((rows, 128), F32),
        pltpu.VMEM((half, 128), F32),
        pltpu.VMEM((16, half, 128), F32),
        pltpu.VMEM((8, half, 128), F32),
        pltpu.VMEM((rows, 128), F32),
        pltpu.SemaphoreType.DMA((4,)),
        pltpu.SemaphoreType.DMA((4,)),
    ]


def total(scratch):
    xbuf, pbuf, xybuf, zbuf, fin, ss, rs = scratch
    row, col, prow = place()
    core = lax.rem(row, 2)
    z = row // 2
    half = pbuf.shape[0]
    mine = pl.ds(pl.multiple_of(core * half, half), half)
    other = pl.ds(pl.multiple_of((1 - core) * half, half), half)
    cp = pltpu.make_async_remote_copy(
        xbuf.at[other], pbuf, ss.at[0], rs.at[0], device_id=(prow, col), device_id_type=MESH
    )
    cp.start()
    cp.wait()
    xybuf[col] = xbuf[mine, :] + pbuf[...]

    def send_xy(i, c):
        pltpu.make_async_remote_copy(
            xybuf.at[col], xybuf.at[col], ss.at[1], rs.at[1],
            device_id=(row, lax.rem(col + i, 16)), device_id_type=MESH,
        ).start()
        return c

    lax.fori_loop(1, 16, send_xy, 0)
    w = pltpu.make_async_remote_copy(
        xybuf.at[pl.ds(0, 15)], xybuf.at[pl.ds(0, 15)], ss.at[1], rs.at[1],
        device_id=(prow, col), device_id_type=MESH,
    )
    w.wait_recv()
    w.wait_send()
    zbuf[z] = jnp.sum(xybuf[...], axis=0)

    def send_z(i, c):
        pltpu.make_async_remote_copy(
            zbuf.at[z], zbuf.at[z], ss.at[2], rs.at[2],
            device_id=(lax.rem(row + 2 * i, 16), col), device_id_type=MESH,
        ).start()
        return c

    lax.fori_loop(1, 8, send_z, 0)
    w = pltpu.make_async_remote_copy(
        zbuf.at[pl.ds(0, 7)], zbuf.at[pl.ds(0, 7)], ss.at[2], rs.at[2],
        device_id=(prow, col), device_id_type=MESH,
    )
    w.wait_recv()
    w.wait_send()
    fin[mine, :] = jnp.sum(zbuf[...], axis=0)
    cp = pltpu.make_async_remote_copy(
        fin.at[mine], fin.at[mine], ss.at[3], rs.at[3], device_id=(prow, col), device_id_type=MESH
    )
    cp.start()
    cp.wait()
    return fin[...]


def nt(a, b):
    return lax.dot_general(a, b, (((1,), (1,)), ((), ())), precision=HIGHEST, preferred_element_type=F32)


def nn(a, b):
    return lax.dot_general(a, b, (((1,), (0,)), ((), ())), precision=HIGHEST, preferred_element_type=F32)


def wide(ref):
    return jnp.concatenate([ref[t] for t in range(RT)], axis=1)


def put_wide(ref, x):
    for t in range(RT):
        ref[t] = x[:, t * TILE:(t + 1) * TILE].astype(ref.dtype)


def fold(g):
    return jnp.concatenate([g[:32], g[32:]], axis=1)


def unfold(p):
    return jnp.concatenate([p[:, :64], p[:, 64:]], axis=0)


def inverse_factor(g):
    lane = lax.broadcasted_iota(jnp.int32, (8, 128), 1)
    sub = lax.broadcasted_iota(jnp.int32, (8, 128), 0)
    wide_g = jnp.concatenate([g, jnp.zeros((64, 64), F32)], axis=1)
    blocks = [
        jnp.where(lane == sub + (64 + 8 * b), 1.0, wide_g[8 * b:8 * b + 8]) for b in range(8)
    ]
    for j in range(0, 64, 2):
        jb, jr = divmod(j, 8)
        c1 = [jnp.broadcast_to(blocks[b][:, j:j + 1], (8, 128)) for b in range(jb, 8)]
        c2 = [jnp.broadcast_to(blocks[b][:, j + 1:j + 2], (8, 128)) for b in range(jb, 8)]
        r1 = blocks[jb][jr:jr + 1, :]
        ia = 1.0 / c1[0][jr:jr + 1, :]
        ratio = c1[0][jr + 1:jr + 2, :] * ia
        r2 = blocks[jb][jr + 1:jr + 2, :] - ratio * r1
        w2 = r2 / (c2[0][jr + 1:jr + 2, :] - ratio * c1[0][jr + 1:jr + 2, :])
        w1 = r1 * ia - ratio * w2
        for b in range(jb, 8):
            new = blocks[b] - (c1[b - jb] * w1 + c2[b - jb] * w2)
            if b == jb:
                new = jnp.where(sub > jr + 1, new, jnp.where(sub == jr + 1, r2, blocks[b]))
            blocks[b] = new
    out = []
    for b in range(8):
        d = jnp.sum(jnp.where(lane == sub + 8 * b, blocks[b], 0.0), axis=1, keepdims=True)
        out.append(blocks[b][:, 64:] / jnp.sqrt(d))
    return jnp.concatenate(out, axis=0)


def swap_matrix():
    k = lax.broadcasted_iota(jnp.int32, (512, 512), 0)
    n = lax.broadcasted_iota(jnp.int32, (512, 512), 1)
    goal = lax.rem(k // 32, 4) * 128 + (k // 128) * 32 + lax.rem(k, 32)
    return jnp.where(goal == n, 1.0, 0.0).astype(BF16)


def send_halo(q_ref, l_ref, t_ref, h_ref, scratch):
    lhs, swap, out, ss, rs, ls = scratch
    row, col, prow = place()
    me = row * 16 + col
    for t in range(RT):
        lhs[64 * (t // 2):64 * (t // 2) + 64, 128 * (t % 2):128 * (t % 2) + 128] = q_ref[t].astype(BF16)
    node = lax.broadcasted_iota(jnp.int32, (256, 256), 0)

    def target(i, h):
        return lax.rem(row + 8 + 5 * (2 * i + h), 16)

    def send(i):
        for h in range(2):
            r2 = target(i, h)
            for u in range(16):
                there = r2 * 16 + u

                @pl.when(there != me)
                def _():
                    pltpu.make_async_remote_copy(
                        out.at[there], h_ref.at[me], ss, rs, device_id=(r2, u), device_id_type=MESH
                    ).start()

    def chunk(i, carry):
        parts = []
        for e in range(4):
            c = 4 * target(i, e // 2) + 2 * (e % 2)
            lsel = jnp.concatenate([l_ref[pl.ds(c, 1), :], l_ref[pl.ds(c + 1, 1), :]], axis=1)
            tsel = jnp.concatenate([t_ref[pl.ds(c, 1), :], t_ref[pl.ds(c + 1, 1), :]], axis=1)
            hot = jnp.where(node == lsel, 1.0, 0.0).astype(BF16)
            r = jnp.dot(lhs[...], hot, preferred_element_type=F32)
            acc = jnp.zeros((64, 256), F32)
            for t in range(8):
                acc = acc + jnp.where(tsel == t, r[64 * t:64 * t + 64], 0.0)
            acc = acc.astype(BF16)
            for h in range(2):
                parts.append(
                    jnp.concatenate([acc[16 * g:16 * g + 16, 128 * h:128 * h + 128] for g in range(4)], axis=1)
                )
        msgs = jnp.dot(jnp.concatenate(parts, axis=0), swap[...], preferred_element_type=F32).astype(BF16)
        for h in range(2):
            first = 16 * target(i, h)
            for v in range(4):
                for q in range(4):
                    u = 4 * h + v
                    out[first + 4 * v + q] = msgs[16 * u:16 * u + 16, 128 * q:128 * q + 128]

        @pl.when(i > 0)
        def _():
            send(i - 1)

        return carry

    lax.fori_loop(0, 8, chunk, 0)
    send(7)
    own = pltpu.make_async_copy(out.at[me], h_ref.at[me], ls)
    own.start()
    w = pltpu.make_async_remote_copy(
        out.at[pl.ds(0, 255)], h_ref.at[pl.ds(0, 255)], ss, rs,
        device_id=(prow, col), device_id_type=MESH,
    )
    w.wait_recv()
    w.wait_send()
    own.wait()


def halo_scratch():
    return [
        pltpu.VMEM((512, 256), BF16),
        pltpu.VMEM((512, 512), BF16),
        pltpu.VMEM((DEVS, 16, 128), BF16),
        pltpu.SemaphoreType.DMA,
        pltpu.SemaphoreType.DMA,
        pltpu.SemaphoreType.DMA,
    ]


def normalize(z, total_gram, q_ref, p_ref):
    m = inverse_factor(unfold(total_gram) * (1.0 / NODES))
    put_wide(q_ref, nn(m, z))
    p_ref[...] = q_ref[...].astype(BF16)


def first_kernel(x_ref, l_ref, t_ref, q_ref, p_ref, h_ref, *scratch):
    greet()
    x = wide(x_ref)
    scratch[0][...] = fold(nt(x, x))
    scratch[8][...] = swap_matrix()
    greeted()
    g = total(scratch[:7])
    normalize(wide(x_ref), g, q_ref, p_ref)
    send_halo(q_ref, l_ref, t_ref, h_ref, scratch[7:])


def residual(nb, y_ref, basis, c, z_ref):
    z = wide(y_ref)
    for i, b in enumerate(basis):
        z = z - nn(unfold(c[32 * i:32 * i + 32]) * (1.0 / NODES), wide(b))
    put_wide(z_ref, z)
    return fold(nt(z, z))


def next_kernel(y_ref, c_ref, q0_ref, l_ref, t_ref, q_ref, p_ref, h_ref, z_ref, *scratch):
    greet()
    scratch[0][...] = c_ref[...]
    scratch[15][...] = swap_matrix()
    greeted()
    c = total(scratch[:7])
    scratch[7][...] = residual(1, y_ref, [q0_ref], c, z_ref)
    g = total(scratch[7:14])
    normalize(wide(z_ref), g, q_ref, p_ref)
    send_halo(q_ref, l_ref, t_ref, h_ref, scratch[14:])


def last_kernel(y_ref, c_ref, q0_ref, q1_ref, rot_ref, o_ref, z_ref, *scratch):
    greet()
    scratch[0][...] = c_ref[...]
    rot = rot_ref[...]
    greeted()
    c = total(scratch[:7])
    scratch[7][...] = residual(2, y_ref, [q0_ref, q1_ref], c, z_ref)
    g = total(scratch[7:14])
    m = inverse_factor(unfold(g) * (1.0 / NODES))
    tail = nn(rot[:, 128:192], m)
    o = nn(rot[:, 0:64], wide(q0_ref)) + nn(rot[:, 64:128], wide(q1_ref)) + nn(tail, wide(z_ref))
    put_wide(o_ref, o)


def apply_kernel(nb, *refs):
    rows, cols, count, values, p_ref, h_ref = refs[:6]
    basis = refs[6:6 + nb]
    y_ref, c_ref, src, acc, swap, buf, sem = refs[6 + nb:]
    n = count[0]
    nchunk = (n + CHUNK - 1) // CHUNK

    def fetch(c):
        part = pl.ds(c * CHUNK, CHUNK)
        return pltpu.make_async_copy(values.at[part], buf.at[part], sem.at[c])

    def begin(c, carry):
        fetch(c).start()
        return carry

    lax.fori_loop(0, nchunk, begin, 0)
    acc[...] = jnp.zeros_like(acc)
    src[0:RT] = p_ref[...]
    swap[...] = swap_matrix()

    def unpack(h, carry):
        parts = [
            jnp.concatenate([h_ref[32 * h + 4 * u + q] for q in range(4)], axis=1) for u in range(8)
        ]
        tiles = jnp.dot(jnp.concatenate(parts, axis=0), swap[...], preferred_element_type=F32).astype(BF16)
        for u in range(8):
            for g in range(4):
                src[RT + 8 * h + u, 16 * g:16 * g + 16, :] = tiles[16 * u:16 * u + 16, 128 * g:128 * g + 128]
        return carry

    lax.fori_loop(0, 8, unpack, 0)

    def step(c, carry):
        fetch(c).wait()
        for u in range(CHUNK):
            k = c * CHUNK + u
            r = jnp.where(k < n, rows[k], RT)
            acc[r] += lax.dot_general(
                src[cols[k]], buf[k], (((1,), (1,)), ((), ())), preferred_element_type=F32
            )
        return carry

    lax.fori_loop(0, nchunk, step, 0)
    y_ref[...] = acc[0:RT]
    y = wide(acc)
    c_ref[...] = jnp.concatenate([fold(nt(y, wide(b))) for b in basis], axis=0)


def block(dtype):
    return jax.ShapeDtypeStruct((RT, BLK, TILE), dtype)


def remote(kernel, cid, outs, scratch, *operands):
    return pl.pallas_call(
        kernel,
        out_shape=outs,
        in_specs=[VMEM] * len(operands),
        out_specs=(VMEM,) * len(outs),
        scratch_shapes=scratch,
        compiler_params=pltpu.CompilerParams(collective_id=cid, has_side_effects=True),
    )(*operands)


def apply_graph(rows, cols, count, values, p, halo, basis):
    nb = len(basis)
    return pl.pallas_call(
        functools.partial(apply_kernel, nb),
        out_shape=(block(F32), jax.ShapeDtypeStruct((32 * nb, 128), F32)),
        in_specs=[SMEM] * 3 + [pl.BlockSpec(memory_space=pl.ANY)] + [VMEM] * (2 + nb),
        out_specs=(VMEM,) * 2,
        scratch_shapes=[
            pltpu.VMEM((80, BLK, TILE), BF16),
            pltpu.VMEM((RT + 1, BLK, TILE), F32),
            pltpu.VMEM((512, 512), BF16),
            pltpu.VMEM((DEVS, TILE, TILE), BF16),
            pltpu.SemaphoreType.DMA((DEVS // CHUNK,)),
        ],
    )(rows, cols, count, values, p, halo, *basis)


def body(start, values, rows, cols, count, send_rows, send_count, rotation):
    slot = jnp.arange(32, dtype=jnp.int32)
    wanted = send_rows[0]
    lsel = (wanted % 256).reshape(64, 128)
    tsel = jnp.where(slot[None, :] < send_count[0][:, None], wanted // 256, -1).reshape(64, 128)
    state = (block(F32), block(BF16), jax.ShapeDtypeStruct((DEVS, 16, 128), BF16))
    held = [pltpu.VMEM((RT, BLK, TILE), F32)]
    q0, p, halo = remote(first_kernel, 1, state, sum_scratch(32) + halo_scratch(), start, lsel, tsel)
    y, c = apply_graph(rows, cols, count, values, p, halo, [q0])
    q1, p, halo = remote(
        next_kernel, 2, state, held + sum_scratch(32) + sum_scratch(32) + halo_scratch(), y, c, q0, lsel, tsel
    )
    y, c = apply_graph(rows, cols, count, values, p, halo, [q0, q1])
    return remote(
        last_kernel, 3, (block(F32),), held + sum_scratch(64) + sum_scratch(32), y, c, q0, q1, rotation.T
    )[0]


def solution(mesh):
    spec = P(("row", "col"))
    return jax.shard_map(
        body,
        mesh=mesh,
        in_specs=(spec,) * 7 + (P(),),
        out_specs=spec,
        check_vma=False,
    )
```

```python
import functools

import jax
import jax.numpy as jnp
from jax import lax
from jax.experimental import pallas as pl
from jax.experimental.pallas import tpu as pltpu
from jax.sharding import PartitionSpec as P

MESH = pl.DeviceIdType.MESH
HIGHEST = lax.Precision.HIGHEST
F32 = jnp.float32
BF16 = jnp.bfloat16
RT = 16
BLK = 64
TILE = 128
DEVS = 256
NODES = 524288
CHUNK = 16
VMEM = pl.BlockSpec(memory_space=pltpu.VMEM)
SMEM = pl.BlockSpec(memory_space=pltpu.SMEM)


def place():
    row = lax.axis_index("row")
    col = lax.axis_index("col")
    return row, col, row + 1 - 2 * lax.rem(row, 2)


def greet():
    row, col, prow = place()
    bar = pltpu.get_barrier_semaphore()
    pl.semaphore_signal(bar, inc=1, device_id=(prow, col), device_id_type=MESH)

    def greet_xy(i, c):
        pl.semaphore_signal(bar, inc=1, device_id=(row, lax.rem(col + i, 16)), device_id_type=MESH)
        return c

    lax.fori_loop(1, 16, greet_xy, 0)

    def greet_z(i, c):
        pl.semaphore_signal(bar, inc=1, device_id=(lax.rem(row + 2 * i, 16), col), device_id_type=MESH)
        return c

    lax.fori_loop(1, 8, greet_z, 0)


def greeted():
    pl.semaphore_wait(pltpu.get_barrier_semaphore(), 23)


def sum_scratch(rows):
    half = rows // 2
    return [
        pltpu.VMEM((rows, 128), F32),
        pltpu.VMEM((half, 128), F32),
        pltpu.VMEM((16, half, 128), F32),
        pltpu.VMEM((8, half, 128), F32),
        pltpu.VMEM((rows, 128), F32),
        pltpu.SemaphoreType.DMA((4,)),
        pltpu.SemaphoreType.DMA((4,)),
    ]


def total(scratch):
    xbuf, pbuf, xybuf, zbuf, fin, ss, rs = scratch
    row, col, prow = place()
    core = lax.rem(row, 2)
    z = row // 2
    half = pbuf.shape[0]
    mine = pl.ds(pl.multiple_of(core * half, half), half)
    other = pl.ds(pl.multiple_of((1 - core) * half, half), half)
    cp = pltpu.make_async_remote_copy(
        xbuf.at[other], pbuf, ss.at[0], rs.at[0], device_id=(prow, col), device_id_type=MESH
    )
    cp.start()
    cp.wait()
    xybuf[col] = xbuf[mine, :] + pbuf[...]

    def send_xy(i, c):
        pltpu.make_async_remote_copy(
            xybuf.at[col], xybuf.at[col], ss.at[1], rs.at[1],
            device_id=(row, lax.rem(col + i, 16)), device_id_type=MESH,
        ).start()
        return c

    lax.fori_loop(1, 16, send_xy, 0)
    w = pltpu.make_async_remote_copy(
        xybuf.at[pl.ds(0, 15)], xybuf.at[pl.ds(0, 15)], ss.at[1], rs.at[1],
        device_id=(prow, col), device_id_type=MESH,
    )
    w.wait_recv()
    w.wait_send()
    zbuf[z] = jnp.sum(xybuf[...], axis=0)

    def send_z(i, c):
        pltpu.make_async_remote_copy(
            zbuf.at[z], zbuf.at[z], ss.at[2], rs.at[2],
            device_id=(lax.rem(row + 2 * i, 16), col), device_id_type=MESH,
        ).start()
        return c

    lax.fori_loop(1, 8, send_z, 0)
    w = pltpu.make_async_remote_copy(
        zbuf.at[pl.ds(0, 7)], zbuf.at[pl.ds(0, 7)], ss.at[2], rs.at[2],
        device_id=(prow, col), device_id_type=MESH,
    )
    w.wait_recv()
    w.wait_send()
    fin[mine, :] = jnp.sum(zbuf[...], axis=0)
    cp = pltpu.make_async_remote_copy(
        fin.at[mine], fin.at[mine], ss.at[3], rs.at[3], device_id=(prow, col), device_id_type=MESH
    )
    cp.start()
    cp.wait()
    return fin[...]


def nt(a, b):
    return lax.dot_general(a, b, (((1,), (1,)), ((), ())), precision=HIGHEST, preferred_element_type=F32)


def nn(a, b):
    return lax.dot_general(a, b, (((1,), (0,)), ((), ())), precision=HIGHEST, preferred_element_type=F32)


def wide(ref):
    return jnp.concatenate([ref[t] for t in range(RT)], axis=1)


def put_wide(ref, x):
    for t in range(RT):
        ref[t] = x[:, t * TILE:(t + 1) * TILE].astype(ref.dtype)


def fold(g):
    return jnp.concatenate([g[:32], g[32:]], axis=1)


def unfold(p):
    return jnp.concatenate([p[:, :64], p[:, 64:]], axis=0)


def inverse_factor(g):
    lane = lax.broadcasted_iota(jnp.int32, (8, 128), 1)
    sub = lax.broadcasted_iota(jnp.int32, (8, 128), 0)
    wide_g = jnp.concatenate([g, jnp.zeros((64, 64), F32)], axis=1)
    blocks = [
        jnp.where(lane == sub + (64 + 8 * b), 1.0, wide_g[8 * b:8 * b + 8]) for b in range(8)
    ]
    for j in range(0, 64, 2):
        jb, jr = divmod(j, 8)
        c1 = [jnp.broadcast_to(blocks[b][:, j:j + 1], (8, 128)) for b in range(jb, 8)]
        c2 = [jnp.broadcast_to(blocks[b][:, j + 1:j + 2], (8, 128)) for b in range(jb, 8)]
        r1 = blocks[jb][jr:jr + 1, :]
        ia = 1.0 / c1[0][jr:jr + 1, :]
        ratio = c1[0][jr + 1:jr + 2, :] * ia
        r2 = blocks[jb][jr + 1:jr + 2, :] - ratio * r1
        w2 = r2 / (c2[0][jr + 1:jr + 2, :] - ratio * c1[0][jr + 1:jr + 2, :])
        w1 = r1 * ia - ratio * w2
        for b in range(jb, 8):
            new = blocks[b] - (c1[b - jb] * w1 + c2[b - jb] * w2)
            if b == jb:
                new = jnp.where(sub > jr + 1, new, jnp.where(sub == jr + 1, r2, blocks[b]))
            blocks[b] = new
    out = []
    for b in range(8):
        d = jnp.sum(jnp.where(lane == sub + 8 * b, blocks[b], 0.0), axis=1, keepdims=True)
        out.append(blocks[b][:, 64:] / jnp.sqrt(d))
    return jnp.concatenate(out, axis=0)


def swap_matrix():
    k = lax.broadcasted_iota(jnp.int32, (512, 512), 0)
    n = lax.broadcasted_iota(jnp.int32, (512, 512), 1)
    goal = lax.rem(k // 32, 4) * 128 + (k // 128) * 32 + lax.rem(k, 32)
    return jnp.where(goal == n, 1.0, 0.0).astype(BF16)


def send_halo(q_ref, l_ref, t_ref, h_ref, scratch):
    lhs, swap, out, ss, rs, ls = scratch
    row, col, prow = place()
    me = row * 16 + col
    for t in range(RT):
        lhs[64 * (t // 2):64 * (t // 2) + 64, 128 * (t % 2):128 * (t % 2) + 128] = q_ref[t].astype(BF16)
    node = lax.broadcasted_iota(jnp.int32, (256, 256), 0)

    core = lax.rem(row, 2)

    def target(i):
        k = i // 2
        away = (k + 1) // 2
        dz = jnp.where(lax.rem(k, 2) == 1, 4 - away, 4 + away)
        flip = lax.rem(i, 2)
        return 2 * lax.rem(row // 2 + dz, 8) + core + flip - 2 * core * flip

    def send(i):
        r2 = target(i)
        for u in range(16):
            c2 = lax.rem(col + 10 + u, 16)
            there = r2 * 16 + c2

            @pl.when(there != me)
            def _():
                pltpu.make_async_remote_copy(
                    out.at[there], h_ref.at[me], ss, rs, device_id=(r2, c2), device_id_type=MESH
                ).start()

    def chunk(i, carry):
        parts = []
        r2 = target(i)
        for e in range(2):
            c = 4 * r2 + 2 * e
            lsel = jnp.concatenate([l_ref[pl.ds(c, 1), :], l_ref[pl.ds(c + 1, 1), :]], axis=1)
            tsel = jnp.concatenate([t_ref[pl.ds(c, 1), :], t_ref[pl.ds(c + 1, 1), :]], axis=1)
            hot = jnp.where(node == lsel, 1.0, 0.0).astype(BF16)
            r = jnp.dot(lhs[...], hot, preferred_element_type=F32)
            acc = jnp.zeros((64, 256), F32)
            for t in range(8):
                acc = acc + jnp.where(tsel == t, r[64 * t:64 * t + 64], 0.0)
            acc = acc.astype(BF16)
            for h in range(2):
                parts.append(
                    jnp.concatenate([acc[16 * g:16 * g + 16, 128 * h:128 * h + 128] for g in range(4)], axis=1)
                )
        msgs = jnp.dot(jnp.concatenate(parts, axis=0), swap[...], preferred_element_type=F32).astype(BF16)
        for v in range(4):
            for q in range(4):
                out[16 * r2 + 4 * v + q] = msgs[16 * v:16 * v + 16, 128 * q:128 * q + 128]

        @pl.when(i > 0)
        def _():
            send(i - 1)

        return carry

    lax.fori_loop(0, 16, chunk, 0)
    send(15)
    own = pltpu.make_async_copy(out.at[me], h_ref.at[me], ls)
    own.start()
    w = pltpu.make_async_remote_copy(
        out.at[pl.ds(0, 255)], h_ref.at[pl.ds(0, 255)], ss, rs,
        device_id=(prow, col), device_id_type=MESH,
    )
    w.wait_recv()
    w.wait_send()
    own.wait()


def halo_scratch():
    return [
        pltpu.VMEM((512, 256), BF16),
        pltpu.VMEM((512, 512), BF16),
        pltpu.VMEM((DEVS, 16, 128), BF16),
        pltpu.SemaphoreType.DMA,
        pltpu.SemaphoreType.DMA,
        pltpu.SemaphoreType.DMA,
    ]


def normalize(z, total_gram, q_ref, p_ref):
    m = inverse_factor(unfold(total_gram) * (1.0 / NODES))
    put_wide(q_ref, nn(m, z))
    p_ref[...] = q_ref[...].astype(BF16)


def index_tables(w_ref, n_ref, l_ref, t_ref):
    wanted = jnp.concatenate([w_ref[pl.ds(q, 64, stride=4), :] for q in range(4)], axis=1)
    dest = lax.broadcasted_iota(jnp.int32, (64, 256), 1)
    group = lax.broadcasted_iota(jnp.int32, (64, 256), 0)
    spread = jnp.where(dest // 4 == group, n_ref[...].astype(F32), 0.0).astype(BF16)
    dest = lax.broadcasted_iota(jnp.int32, (256, 128), 0)
    lane = lax.broadcasted_iota(jnp.int32, (256, 128), 1)
    pick = jnp.where(lax.rem(dest, 4) == lane // 32, 1.0, 0.0).astype(BF16)
    live = jnp.dot(spread, pick, preferred_element_type=F32)
    slot = lax.rem(lax.broadcasted_iota(jnp.int32, (64, 128), 1), 32)
    l_ref[...] = lax.rem(wanted, 256)
    t_ref[...] = jnp.where(slot.astype(F32) < live, wanted // 256, -1)


def first_kernel(x_ref, w_ref, n_ref, q_ref, p_ref, h_ref, l_ref, t_ref, *scratch):
    greet()
    x = wide(x_ref)
    scratch[0][...] = fold(nt(x, x))
    scratch[8][...] = swap_matrix()
    index_tables(w_ref, n_ref, l_ref, t_ref)
    greeted()
    g = total(scratch[:7])
    normalize(wide(x_ref), g, q_ref, p_ref)
    send_halo(q_ref, l_ref, t_ref, h_ref, scratch[7:])


def residual(nb, y_ref, basis, c, z_ref):
    z = wide(y_ref)
    for i, b in enumerate(basis):
        z = z - nn(unfold(c[32 * i:32 * i + 32]) * (1.0 / NODES), wide(b))
    put_wide(z_ref, z)
    return fold(nt(z, z))


def next_kernel(y_ref, c_ref, q0_ref, l_ref, t_ref, q_ref, p_ref, h_ref, z_ref, *scratch):
    greet()
    scratch[0][...] = c_ref[...]
    scratch[15][...] = swap_matrix()
    greeted()
    c = total(scratch[:7])
    scratch[7][...] = residual(1, y_ref, [q0_ref], c, z_ref)
    g = total(scratch[7:14])
    normalize(wide(z_ref), g, q_ref, p_ref)
    send_halo(q_ref, l_ref, t_ref, h_ref, scratch[14:])


def last_kernel(y_ref, c_ref, q0_ref, q1_ref, rot_ref, o_ref, z_ref, *scratch):
    greet()
    scratch[0][...] = c_ref[...]
    rot = rot_ref[...]
    greeted()
    c = total(scratch[:7])
    scratch[7][...] = residual(2, y_ref, [q0_ref, q1_ref], c, z_ref)
    g = total(scratch[7:14])
    m = inverse_factor(unfold(g) * (1.0 / NODES))
    tail = nn(rot[:, 128:192], m)
    o = nn(rot[:, 0:64], wide(q0_ref)) + nn(rot[:, 64:128], wide(q1_ref)) + nn(tail, wide(z_ref))
    put_wide(o_ref, o)


def apply_kernel(nb, *refs):
    rows, cols, count, values, p_ref, h_ref = refs[:6]
    basis = refs[6:6 + nb]
    y_ref, c_ref, src, acc, swap, buf, sem = refs[6 + nb:]
    n = count[0]
    nchunk = (n + CHUNK - 1) // CHUNK

    def fetch(c):
        part = pl.ds(c * CHUNK, CHUNK)
        return pltpu.make_async_copy(values.at[part], buf.at[part], sem.at[c])

    def begin(c, carry):
        fetch(c).start()
        return carry

    lax.fori_loop(0, nchunk, begin, 0)
    acc[...] = jnp.zeros_like(acc)
    src[0:RT] = p_ref[...]
    swap[...] = swap_matrix()

    def unpack(h, carry):
        parts = [
            jnp.concatenate([h_ref[32 * h + 4 * u + q] for q in range(4)], axis=1) for u in range(8)
        ]
        tiles = jnp.dot(jnp.concatenate(parts, axis=0), swap[...], preferred_element_type=F32).astype(BF16)
        for u in range(8):
            for g in range(4):
                src[RT + 8 * h + u, 16 * g:16 * g + 16, :] = tiles[16 * u:16 * u + 16, 128 * g:128 * g + 128]
        return carry

    lax.fori_loop(0, 8, unpack, 0)

    def step(c, carry):
        fetch(c).wait()
        for u in range(CHUNK):
            k = c * CHUNK + u
            r = jnp.where(k < n, rows[k], RT)
            acc[r] += lax.dot_general(
                src[cols[k]], buf[k], (((1,), (1,)), ((), ())), preferred_element_type=F32
            )
        return carry

    lax.fori_loop(0, nchunk, step, 0)
    y_ref[...] = acc[0:RT]
    y = wide(acc)
    c_ref[...] = jnp.concatenate([fold(nt(y, wide(b))) for b in basis], axis=0)


def block(dtype):
    return jax.ShapeDtypeStruct((RT, BLK, TILE), dtype)


def remote(kernel, cid, outs, scratch, *operands):
    return pl.pallas_call(
        kernel,
        out_shape=outs,
        in_specs=[VMEM] * len(operands),
        out_specs=(VMEM,) * len(outs),
        scratch_shapes=scratch,
        compiler_params=pltpu.CompilerParams(
            collective_id=cid, has_side_effects=True, vmem_limit_bytes=24 * 1024 * 1024
        ),
    )(*operands)


def apply_graph(rows, cols, count, values, p, halo, basis):
    nb = len(basis)
    return pl.pallas_call(
        functools.partial(apply_kernel, nb),
        out_shape=(block(F32), jax.ShapeDtypeStruct((32 * nb, 128), F32)),
        in_specs=[SMEM] * 3 + [pl.BlockSpec(memory_space=pltpu.HBM)] + [VMEM] * (2 + nb),
        out_specs=(VMEM,) * 2,
        scratch_shapes=[
            pltpu.VMEM((80, BLK, TILE), BF16),
            pltpu.VMEM((RT + 1, BLK, TILE), F32),
            pltpu.VMEM((512, 512), BF16),
            pltpu.VMEM((DEVS, TILE, TILE), BF16),
            pltpu.SemaphoreType.DMA((DEVS // CHUNK,)),
        ],
        compiler_params=pltpu.CompilerParams(vmem_limit_bytes=24 * 1024 * 1024),
    )(rows, cols, count, values, p, halo, *basis)


def body(start, values, rows, cols, count, send_rows, send_count, rotation):
    state = (block(F32), block(BF16), jax.ShapeDtypeStruct((DEVS, 16, 128), BF16))
    held = [pltpu.VMEM((RT, BLK, TILE), F32)]
    table = jax.ShapeDtypeStruct((64, 128), jnp.int32)
    q0, p, halo, lsel, tsel = remote(
        first_kernel, 1, state + (table, table), sum_scratch(32) + halo_scratch(), start, send_rows[0], send_count
    )
    y, c = apply_graph(rows, cols, count, values, p, halo, [q0])
    q1, p, halo = remote(
        next_kernel, 2, state, held + sum_scratch(32) + sum_scratch(32) + halo_scratch(), y, c, q0, lsel, tsel
    )
    y, c = apply_graph(rows, cols, count, values, p, halo, [q0, q1])
    return remote(
        last_kernel, 3, (block(F32),), held + sum_scratch(64) + sum_scratch(32), y, c, q0, q1, rotation.T
    )[0]


def solution(mesh):
    spec = P(("row", "col"))
    return jax.shard_map(
        body,
        mesh=mesh,
        in_specs=(spec,) * 7 + (P(),),
        out_specs=spec,
        check_vma=False,
    )
```

```python
import functools

import jax
import jax.numpy as jnp
from jax import lax
from jax.experimental import pallas as pl
from jax.experimental.pallas import tpu as pltpu
from jax.sharding import PartitionSpec as P

MESH = pl.DeviceIdType.MESH
HIGHEST = lax.Precision.HIGHEST
F32 = jnp.float32
BF16 = jnp.bfloat16
RT = 16
BLK = 64
TILE = 128
DEVS = 256
NODES = 524288
CHUNK = 16
VMEM = pl.BlockSpec(memory_space=pltpu.VMEM)
SMEM = pl.BlockSpec(memory_space=pltpu.SMEM)


def place():
    row = lax.axis_index("row")
    col = lax.axis_index("col")
    return row, col, row + 1 - 2 * lax.rem(row, 2)


def greet():
    row, col, prow = place()
    bar = pltpu.get_barrier_semaphore()
    pl.semaphore_signal(bar, inc=1, device_id=(prow, col), device_id_type=MESH)

    def greet_xy(i, c):
        pl.semaphore_signal(bar, inc=1, device_id=(row, lax.rem(col + i, 16)), device_id_type=MESH)
        return c

    lax.fori_loop(1, 16, greet_xy, 0)

    def greet_z(i, c):
        pl.semaphore_signal(bar, inc=1, device_id=(lax.rem(row + 2 * i, 16), col), device_id_type=MESH)
        return c

    lax.fori_loop(1, 8, greet_z, 0)


def greeted():
    pl.semaphore_wait(pltpu.get_barrier_semaphore(), 23)


def sum_scratch(rows):
    half = rows // 2
    return [
        pltpu.VMEM((rows, 128), F32),
        pltpu.VMEM((half, 128), F32),
        pltpu.VMEM((16, half, 128), F32),
        pltpu.VMEM((8, half, 128), F32),
        pltpu.VMEM((rows, 128), F32),
        pltpu.SemaphoreType.DMA((4,)),
        pltpu.SemaphoreType.DMA((4,)),
    ]


def total(scratch, during=None):
    xbuf, pbuf, xybuf, zbuf, fin, ss, rs = scratch
    row, col, prow = place()
    core = lax.rem(row, 2)
    z = row // 2
    half = pbuf.shape[0]
    mine = pl.ds(pl.multiple_of(core * half, half), half)
    other = pl.ds(pl.multiple_of((1 - core) * half, half), half)
    cp = pltpu.make_async_remote_copy(
        xbuf.at[other], pbuf, ss.at[0], rs.at[0], device_id=(prow, col), device_id_type=MESH
    )
    cp.start()
    cp.wait()
    xybuf[col] = xbuf[mine, :] + pbuf[...]

    def send_xy(i, c):
        pltpu.make_async_remote_copy(
            xybuf.at[col], xybuf.at[col], ss.at[1], rs.at[1],
            device_id=(row, lax.rem(col + i, 16)), device_id_type=MESH,
        ).start()
        return c

    lax.fori_loop(1, 16, send_xy, 0)
    if during is not None:
        during()
    w = pltpu.make_async_remote_copy(
        xybuf.at[pl.ds(0, 15)], xybuf.at[pl.ds(0, 15)], ss.at[1], rs.at[1],
        device_id=(prow, col), device_id_type=MESH,
    )
    w.wait_recv()
    w.wait_send()
    zbuf[z] = jnp.sum(xybuf[...], axis=0)

    def send_z(i, c):
        pltpu.make_async_remote_copy(
            zbuf.at[z], zbuf.at[z], ss.at[2], rs.at[2],
            device_id=(lax.rem(row + 2 * i, 16), col), device_id_type=MESH,
        ).start()
        return c

    lax.fori_loop(1, 8, send_z, 0)
    w = pltpu.make_async_remote_copy(
        zbuf.at[pl.ds(0, 7)], zbuf.at[pl.ds(0, 7)], ss.at[2], rs.at[2],
        device_id=(prow, col), device_id_type=MESH,
    )
    w.wait_recv()
    w.wait_send()
    fin[mine, :] = jnp.sum(zbuf[...], axis=0)
    cp = pltpu.make_async_remote_copy(
        fin.at[mine], fin.at[mine], ss.at[3], rs.at[3], device_id=(prow, col), device_id_type=MESH
    )
    cp.start()
    cp.wait()
    return fin[...]


def nt(a, b):
    return lax.dot_general(a, b, (((1,), (1,)), ((), ())), precision=HIGHEST, preferred_element_type=F32)


def nn(a, b):
    return lax.dot_general(a, b, (((1,), (0,)), ((), ())), precision=HIGHEST, preferred_element_type=F32)


def wide(ref):
    return jnp.concatenate([ref[t] for t in range(RT)], axis=1)


def put_wide(ref, x):
    for t in range(RT):
        ref[t] = x[:, t * TILE:(t + 1) * TILE].astype(ref.dtype)


def fold(g):
    return jnp.concatenate([g[:32], g[32:]], axis=1)


def unfold(p):
    return jnp.concatenate([p[:, :64], p[:, 64:]], axis=0)


def inverse_factor(g):
    lane = lax.broadcasted_iota(jnp.int32, (8, 128), 1)
    sub = lax.broadcasted_iota(jnp.int32, (8, 128), 0)
    wide_g = jnp.concatenate([g, jnp.zeros((64, 64), F32)], axis=1)
    blocks = [
        jnp.where(lane == sub + (64 + 8 * b), 1.0, wide_g[8 * b:8 * b + 8]) for b in range(8)
    ]
    for j in range(0, 64, 2):
        jb, jr = divmod(j, 8)
        c1 = [jnp.broadcast_to(blocks[b][:, j:j + 1], (8, 128)) for b in range(jb, 8)]
        c2 = [jnp.broadcast_to(blocks[b][:, j + 1:j + 2], (8, 128)) for b in range(jb, 8)]
        r1 = blocks[jb][jr:jr + 1, :]
        ia = 1.0 / c1[0][jr:jr + 1, :]
        ratio = c1[0][jr + 1:jr + 2, :] * ia
        r2 = blocks[jb][jr + 1:jr + 2, :] - ratio * r1
        w2 = r2 / (c2[0][jr + 1:jr + 2, :] - ratio * c1[0][jr + 1:jr + 2, :])
        w1 = r1 * ia - ratio * w2
        for b in range(jb, 8):
            new = blocks[b] - (c1[b - jb] * w1 + c2[b - jb] * w2)
            if b == jb:
                new = jnp.where(sub > jr + 1, new, jnp.where(sub == jr + 1, r2, blocks[b]))
            blocks[b] = new
    out = []
    for b in range(8):
        d = jnp.sum(jnp.where(lane == sub + 8 * b, blocks[b], 0.0), axis=1, keepdims=True)
        out.append(blocks[b][:, 64:] / jnp.sqrt(d))
    return jnp.concatenate(out, axis=0)


def swap_matrix():
    k = lax.broadcasted_iota(jnp.int32, (512, 512), 0)
    n = lax.broadcasted_iota(jnp.int32, (512, 512), 1)
    goal = lax.rem(k // 32, 4) * 128 + (k // 128) * 32 + lax.rem(k, 32)
    return jnp.where(goal == n, 1.0, 0.0).astype(BF16)


def send_halo(q_ref, l_ref, t_ref, h_ref, scratch):
    lhs, swap, out, ss, rs, ls = scratch
    row, col, prow = place()
    me = row * 16 + col
    for t in range(RT):
        lhs[64 * (t // 2):64 * (t // 2) + 64, 128 * (t % 2):128 * (t % 2) + 128] = q_ref[t].astype(BF16)
    node = lax.broadcasted_iota(jnp.int32, (256, 256), 0)

    core = lax.rem(row, 2)

    def target(i):
        k = i // 2
        away = (k + 1) // 2
        dz = jnp.where(lax.rem(k, 2) == 1, 4 - away, 4 + away)
        flip = lax.rem(i, 2)
        return 2 * lax.rem(row // 2 + dz, 8) + core + flip - 2 * core * flip

    def send(i):
        r2 = target(i)
        for u in range(16):
            c2 = lax.rem(col + 10 + u, 16)
            there = r2 * 16 + c2

            @pl.when(there != me)
            def _():
                pltpu.make_async_remote_copy(
                    out.at[there], h_ref.at[me], ss, rs, device_id=(r2, c2), device_id_type=MESH
                ).start()

    def chunk(i, carry):
        parts = []
        r2 = target(i)
        for e in range(2):
            c = 4 * r2 + 2 * e
            lsel = jnp.concatenate([l_ref[pl.ds(c, 1), :], l_ref[pl.ds(c + 1, 1), :]], axis=1)
            tsel = jnp.concatenate([t_ref[pl.ds(c, 1), :], t_ref[pl.ds(c + 1, 1), :]], axis=1)
            hot = jnp.where(node == lsel, 1.0, 0.0).astype(BF16)
            r = jnp.dot(lhs[...], hot, preferred_element_type=F32)
            acc = jnp.zeros((64, 256), F32)
            for t in range(8):
                acc = acc + jnp.where(tsel == t, r[64 * t:64 * t + 64], 0.0)
            acc = acc.astype(BF16)
            for h in range(2):
                parts.append(
                    jnp.concatenate([acc[16 * g:16 * g + 16, 128 * h:128 * h + 128] for g in range(4)], axis=1)
                )
        msgs = jnp.dot(jnp.concatenate(parts, axis=0), swap[...], preferred_element_type=F32).astype(BF16)
        for v in range(4):
            for q in range(4):
                out[16 * r2 + 4 * v + q] = msgs[16 * v:16 * v + 16, 128 * q:128 * q + 128]

        @pl.when(i > 0)
        def _():
            send(i - 1)

        return carry

    lax.fori_loop(0, 16, chunk, 0)
    send(15)
    own = pltpu.make_async_copy(out.at[me], h_ref.at[me], ls)
    own.start()
    w = pltpu.make_async_remote_copy(
        out.at[pl.ds(0, 255)], h_ref.at[pl.ds(0, 255)], ss, rs,
        device_id=(prow, col), device_id_type=MESH,
    )
    w.wait_recv()
    w.wait_send()
    own.wait()


def halo_scratch():
    return [
        pltpu.VMEM((512, 256), BF16),
        pltpu.VMEM((512, 512), BF16),
        pltpu.VMEM((DEVS, 16, 128), BF16),
        pltpu.SemaphoreType.DMA,
        pltpu.SemaphoreType.DMA,
        pltpu.SemaphoreType.DMA,
    ]


def normalize(z, total_gram, q_ref, p_ref):
    m = inverse_factor(unfold(total_gram) * (1.0 / NODES))
    put_wide(q_ref, nn(m, z))
    p_ref[...] = q_ref[...].astype(BF16)


def index_tables(w_ref, n_ref, l_ref, t_ref):
    wanted = jnp.concatenate([w_ref[pl.ds(q, 64, stride=4), :] for q in range(4)], axis=1)
    dest = lax.broadcasted_iota(jnp.int32, (64, 256), 1)
    group = lax.broadcasted_iota(jnp.int32, (64, 256), 0)
    spread = jnp.where(dest // 4 == group, n_ref[...].astype(F32), 0.0).astype(BF16)
    dest = lax.broadcasted_iota(jnp.int32, (256, 128), 0)
    lane = lax.broadcasted_iota(jnp.int32, (256, 128), 1)
    pick = jnp.where(lax.rem(dest, 4) == lane // 32, 1.0, 0.0).astype(BF16)
    live = jnp.dot(spread, pick, preferred_element_type=F32)
    slot = lax.rem(lax.broadcasted_iota(jnp.int32, (64, 128), 1), 32)
    l_ref[...] = lax.rem(wanted, 256)
    t_ref[...] = jnp.where(slot.astype(F32) < live, wanted // 256, -1)


def first_kernel(x_ref, w_ref, n_ref, q_ref, p_ref, h_ref, l_ref, t_ref, *scratch):
    greet()
    x = wide(x_ref)
    scratch[0][...] = fold(nt(x, x))
    greeted()

    def during():
        scratch[8][...] = swap_matrix()
        index_tables(w_ref, n_ref, l_ref, t_ref)

    g = total(scratch[:7], during)
    normalize(wide(x_ref), g, q_ref, p_ref)
    send_halo(q_ref, l_ref, t_ref, h_ref, scratch[7:])


def residual(nb, y_ref, basis, c, z_ref):
    z = wide(y_ref)
    for i, b in enumerate(basis):
        z = z - nn(unfold(c[32 * i:32 * i + 32]) * (1.0 / NODES), wide(b))
    put_wide(z_ref, z)
    return fold(nt(z, z))


def next_kernel(y_ref, c_ref, q0_ref, l_ref, t_ref, q_ref, p_ref, h_ref, z_ref, *scratch):
    greet()
    scratch[0][...] = c_ref[...]
    greeted()

    def during():
        scratch[15][...] = swap_matrix()

    c = total(scratch[:7], during)
    scratch[7][...] = residual(1, y_ref, [q0_ref], c, z_ref)
    g = total(scratch[7:14])
    normalize(wide(z_ref), g, q_ref, p_ref)
    send_halo(q_ref, l_ref, t_ref, h_ref, scratch[14:])


def last_kernel(y_ref, c_ref, q0_ref, q1_ref, rot_ref, o_ref, z_ref, *scratch):
    greet()
    scratch[0][...] = c_ref[...]
    rot = rot_ref[...]
    greeted()

    def during():
        put_wide(o_ref, nn(rot[:, 0:64], wide(q0_ref)) + nn(rot[:, 64:128], wide(q1_ref)))

    c = total(scratch[:7], during)
    scratch[7][...] = residual(2, y_ref, [q0_ref, q1_ref], c, z_ref)
    g = total(scratch[7:14])
    m = inverse_factor(unfold(g) * (1.0 / NODES))
    tail = nn(rot[:, 128:192], m)
    put_wide(o_ref, wide(o_ref) + nn(tail, wide(z_ref)))


def apply_kernel(nb, *refs):
    rows, cols, count, values, p_ref, h_ref = refs[:6]
    basis = refs[6:6 + nb]
    y_ref, c_ref, src, acc, swap = refs[6 + nb:]
    n = count[0]
    nchunk = (n + CHUNK - 1) // CHUNK

    acc[...] = jnp.zeros_like(acc)
    src[0:RT] = p_ref[...]
    swap[...] = swap_matrix()

    def unpack(h, carry):
        parts = [
            jnp.concatenate([h_ref[32 * h + 4 * u + q] for q in range(4)], axis=1) for u in range(8)
        ]
        tiles = jnp.dot(jnp.concatenate(parts, axis=0), swap[...], preferred_element_type=F32).astype(BF16)
        for u in range(8):
            for g in range(4):
                src[RT + 8 * h + u, 16 * g:16 * g + 16, :] = tiles[16 * u:16 * u + 16, 128 * g:128 * g + 128]
        return carry

    lax.fori_loop(0, 8, unpack, 0)

    def step(c, carry):
        for u in range(CHUNK):
            k = c * CHUNK + u
            r = jnp.where(k < n, rows[k], RT)
            acc[r] += lax.dot_general(
                src[cols[k]], values[k], (((1,), (1,)), ((), ())), preferred_element_type=F32
            )
        return carry

    lax.fori_loop(0, nchunk, step, 0)
    y_ref[...] = acc[0:RT]
    y = wide(acc)
    c_ref[...] = jnp.concatenate([fold(nt(y, wide(b))) for b in basis], axis=0)


def block(dtype):
    return jax.ShapeDtypeStruct((RT, BLK, TILE), dtype)


def remote(kernel, cid, outs, scratch, *operands):
    return pl.pallas_call(
        kernel,
        out_shape=outs,
        in_specs=[VMEM] * len(operands),
        out_specs=(VMEM,) * len(outs),
        scratch_shapes=scratch,
        cost_estimate=pl.CostEstimate(flops=20_000_000_000, bytes_accessed=100_000_000, transcendentals=0),
        compiler_params=pltpu.CompilerParams(
            collective_id=cid, has_side_effects=True, vmem_limit_bytes=24 * 1024 * 1024
        ),
    )(*operands)


def apply_graph(rows, cols, count, values, p, halo, basis):
    nb = len(basis)
    return pl.pallas_call(
        functools.partial(apply_kernel, nb),
        out_shape=(block(F32), jax.ShapeDtypeStruct((32 * nb, 128), F32)),
        in_specs=[SMEM] * 3 + [VMEM] * (3 + nb),
        out_specs=(VMEM,) * 2,
        scratch_shapes=[
            pltpu.VMEM((80, BLK, TILE), BF16),
            pltpu.VMEM((RT + 1, BLK, TILE), F32),
            pltpu.VMEM((512, 512), BF16),
        ],
        compiler_params=pltpu.CompilerParams(vmem_limit_bytes=24 * 1024 * 1024),
    )(rows, cols, count, values, p, halo, *basis)


def body(start, values, rows, cols, count, send_rows, send_count, rotation):
    state = (block(F32), block(BF16), jax.ShapeDtypeStruct((DEVS, 16, 128), BF16))
    held = [pltpu.VMEM((RT, BLK, TILE), F32)]
    table = jax.ShapeDtypeStruct((64, 128), jnp.int32)
    q0, p, halo, lsel, tsel = remote(
        first_kernel, 1, state + (table, table), sum_scratch(32) + halo_scratch(), start, send_rows[0], send_count
    )
    y, c = apply_graph(rows, cols, count, values, p, halo, [q0])
    q1, p, halo = remote(
        next_kernel, 2, state, held + sum_scratch(32) + sum_scratch(32) + halo_scratch(), y, c, q0, lsel, tsel
    )
    y, c = apply_graph(rows, cols, count, values, p, halo, [q0, q1])
    return remote(
        last_kernel, 3, (block(F32),), held + sum_scratch(64) + sum_scratch(32), y, c, q0, q1, rotation.T
    )[0]


def solution(mesh):
    spec = P(("row", "col"))
    return jax.shard_map(
        body,
        mesh=mesh,
        in_specs=(spec,) * 7 + (P(),),
        out_specs=spec,
        check_vma=False,
    )
```

```python
import functools

import jax
import jax.numpy as jnp
from jax import lax
from jax.experimental import pallas as pl
from jax.experimental.pallas import tpu as pltpu
from jax.sharding import PartitionSpec as P

MESH = pl.DeviceIdType.MESH
HIGHEST = lax.Precision.HIGHEST
F32 = jnp.float32
BF16 = jnp.bfloat16
RT = 16
BLK = 64
TILE = 128
DEVS = 256
NODES = 524288
CHUNK = 16
VMEM = pl.BlockSpec(memory_space=pltpu.VMEM)
SMEM = pl.BlockSpec(memory_space=pltpu.SMEM)


def place():
    row = lax.axis_index("row")
    col = lax.axis_index("col")
    return row, col, row + 1 - 2 * lax.rem(row, 2)


def greet():
    row, col, prow = place()
    bar = pltpu.get_barrier_semaphore()
    pl.semaphore_signal(bar, inc=1, device_id=(prow, col), device_id_type=MESH)

    def greet_xy(i, c):
        pl.semaphore_signal(bar, inc=1, device_id=(row, lax.rem(col + i, 16)), device_id_type=MESH)
        return c

    lax.fori_loop(1, 16, greet_xy, 0)

    def greet_z(i, c):
        pl.semaphore_signal(bar, inc=1, device_id=(lax.rem(row + 2 * i, 16), col), device_id_type=MESH)
        return c

    lax.fori_loop(1, 8, greet_z, 0)


def greeted():
    pl.semaphore_wait(pltpu.get_barrier_semaphore(), 23)


def greet_all():
    row, col, _ = place()
    bar = pltpu.get_barrier_semaphore()

    def one(i, c):
        pl.semaphore_signal(bar, inc=1, device_id=(row, lax.rem(col + i, 16)), device_id_type=MESH)
        pl.semaphore_signal(bar, inc=1, device_id=(lax.rem(row + i, 16), col), device_id_type=MESH)
        return c

    lax.fori_loop(1, 16, one, 0)


def greeted_all_first(sem):
    row, col, _ = place()
    pl.semaphore_wait(pltpu.get_barrier_semaphore(), 30)

    def one(i, c):
        pl.semaphore_signal(sem, inc=1, device_id=(lax.rem(row + i, 16), col), device_id_type=MESH)
        return c

    lax.fori_loop(1, 16, one, 0)


def greeted_all_second(sem):
    pl.semaphore_wait(sem, 15)


def sum_scratch(rows):
    half = rows // 2
    return [
        pltpu.VMEM((rows, 128), F32),
        pltpu.VMEM((half, 128), F32),
        pltpu.VMEM((16, half, 128), F32),
        pltpu.VMEM((8, half, 128), F32),
        pltpu.VMEM((rows, 128), F32),
        pltpu.SemaphoreType.DMA((4,)),
        pltpu.SemaphoreType.DMA((4,)),
    ]


def total(scratch, during=None):
    xbuf, pbuf, xybuf, zbuf, fin, ss, rs = scratch
    row, col, prow = place()
    core = lax.rem(row, 2)
    z = row // 2
    half = pbuf.shape[0]
    mine = pl.ds(pl.multiple_of(core * half, half), half)
    other = pl.ds(pl.multiple_of((1 - core) * half, half), half)
    cp = pltpu.make_async_remote_copy(
        xbuf.at[other], pbuf, ss.at[0], rs.at[0], device_id=(prow, col), device_id_type=MESH
    )
    cp.start()
    cp.wait()
    xybuf[col] = xbuf[mine, :] + pbuf[...]

    def send_xy(i, c):
        pltpu.make_async_remote_copy(
            xybuf.at[col], xybuf.at[col], ss.at[1], rs.at[1],
            device_id=(row, lax.rem(col + i, 16)), device_id_type=MESH,
        ).start()
        return c

    lax.fori_loop(1, 16, send_xy, 0)
    if during is not None:
        during()
    w = pltpu.make_async_remote_copy(
        xybuf.at[pl.ds(0, 15)], xybuf.at[pl.ds(0, 15)], ss.at[1], rs.at[1],
        device_id=(prow, col), device_id_type=MESH,
    )
    w.wait_recv()
    w.wait_send()
    zbuf[z] = jnp.sum(xybuf[...], axis=0)

    def send_z(i, c):
        pltpu.make_async_remote_copy(
            zbuf.at[z], zbuf.at[z], ss.at[2], rs.at[2],
            device_id=(lax.rem(row + 2 * i, 16), col), device_id_type=MESH,
        ).start()
        return c

    lax.fori_loop(1, 8, send_z, 0)
    w = pltpu.make_async_remote_copy(
        zbuf.at[pl.ds(0, 7)], zbuf.at[pl.ds(0, 7)], ss.at[2], rs.at[2],
        device_id=(prow, col), device_id_type=MESH,
    )
    w.wait_recv()
    w.wait_send()
    fin[mine, :] = jnp.sum(zbuf[...], axis=0)
    cp = pltpu.make_async_remote_copy(
        fin.at[mine], fin.at[mine], ss.at[3], rs.at[3], device_id=(prow, col), device_id_type=MESH
    )
    cp.start()
    cp.wait()
    return fin[...]


def nt(a, b):
    return lax.dot_general(a, b, (((1,), (1,)), ((), ())), precision=HIGHEST, preferred_element_type=F32)


def nn(a, b):
    return lax.dot_general(a, b, (((1,), (0,)), ((), ())), precision=HIGHEST, preferred_element_type=F32)


def wide(ref):
    return jnp.concatenate([ref[t] for t in range(RT)], axis=1)


def put_wide(ref, x):
    for t in range(RT):
        ref[t] = x[:, t * TILE:(t + 1) * TILE].astype(ref.dtype)


def fold(g):
    return jnp.concatenate([g[:32], g[32:]], axis=1)


def unfold(p):
    return jnp.concatenate([p[:, :64], p[:, 64:]], axis=0)


def inverse_factor(g):
    lane = lax.broadcasted_iota(jnp.int32, (8, 128), 1)
    sub = lax.broadcasted_iota(jnp.int32, (8, 128), 0)
    wide_g = jnp.concatenate([g, jnp.zeros((64, 64), F32)], axis=1)
    blocks = [
        jnp.where(lane == sub + (64 + 8 * b), 1.0, wide_g[8 * b:8 * b + 8]) for b in range(8)
    ]
    for j in range(0, 64, 2):
        jb, jr = divmod(j, 8)
        c1 = [jnp.broadcast_to(blocks[b][:, j:j + 1], (8, 128)) for b in range(jb, 8)]
        c2 = [jnp.broadcast_to(blocks[b][:, j + 1:j + 2], (8, 128)) for b in range(jb, 8)]
        r1 = blocks[jb][jr:jr + 1, :]
        ia = 1.0 / c1[0][jr:jr + 1, :]
        ratio = c1[0][jr + 1:jr + 2, :] * ia
        r2 = blocks[jb][jr + 1:jr + 2, :] - ratio * r1
        w2 = r2 / (c2[0][jr + 1:jr + 2, :] - ratio * c1[0][jr + 1:jr + 2, :])
        w1 = r1 * ia - ratio * w2
        for b in range(jb, 8):
            new = blocks[b] - (c1[b - jb] * w1 + c2[b - jb] * w2)
            if b == jb:
                new = jnp.where(sub > jr + 1, new, jnp.where(sub == jr + 1, r2, blocks[b]))
            blocks[b] = new
    out = []
    for b in range(8):
        d = jnp.sum(jnp.where(lane == sub + 8 * b, blocks[b], 0.0), axis=1, keepdims=True)
        out.append(blocks[b][:, 64:] / jnp.sqrt(d))
    return jnp.concatenate(out, axis=0)


def swap_matrix():
    k = lax.broadcasted_iota(jnp.int32, (512, 512), 0)
    n = lax.broadcasted_iota(jnp.int32, (512, 512), 1)
    goal = lax.rem(k // 32, 4) * 128 + (k // 128) * 32 + lax.rem(k, 32)
    return jnp.where(goal == n, 1.0, 0.0).astype(BF16)


def send_halo(q_ref, l_ref, t_ref, h_ref, scratch, ready=None):
    lhs, swap, out, ss, rs, ls = scratch
    row, col, prow = place()
    me = row * 16 + col
    for t in range(RT):
        lhs[64 * (t // 2):64 * (t // 2) + 64, 128 * (t % 2):128 * (t % 2) + 128] = q_ref[t].astype(BF16)
    node = lax.broadcasted_iota(jnp.int32, (256, 256), 0)

    core = lax.rem(row, 2)

    def target(i):
        k = i // 2
        away = (k + 1) // 2
        dz = jnp.where(lax.rem(k, 2) == 1, 4 - away, 4 + away)
        flip = lax.rem(i, 2)
        return 2 * lax.rem(row // 2 + dz, 8) + core + flip - 2 * core * flip

    def send(i):
        r2 = target(i)
        for u in range(16):
            c2 = lax.rem(col + 10 + u, 16)
            there = r2 * 16 + c2

            @pl.when(there != me)
            def _():
                pltpu.make_async_remote_copy(
                    out.at[there], h_ref.at[me], ss, rs, device_id=(r2, c2), device_id_type=MESH
                ).start()

    def chunk(i, carry):
        parts = []
        r2 = target(i)
        for e in range(2):
            c = 4 * r2 + 2 * e
            lsel = jnp.concatenate([l_ref[pl.ds(c, 1), :], l_ref[pl.ds(c + 1, 1), :]], axis=1)
            tsel = jnp.concatenate([t_ref[pl.ds(c, 1), :], t_ref[pl.ds(c + 1, 1), :]], axis=1)
            hot = jnp.where(node == lsel, 1.0, 0.0).astype(BF16)
            r = jnp.dot(lhs[...], hot, preferred_element_type=F32)
            acc = jnp.zeros((64, 256), F32)
            for t in range(8):
                acc = acc + jnp.where(tsel == t, r[64 * t:64 * t + 64], 0.0)
            acc = acc.astype(BF16)
            for h in range(2):
                parts.append(
                    jnp.concatenate([acc[16 * g:16 * g + 16, 128 * h:128 * h + 128] for g in range(4)], axis=1)
                )
        msgs = jnp.dot(jnp.concatenate(parts, axis=0), swap[...], preferred_element_type=F32).astype(BF16)
        for v in range(4):
            for q in range(4):
                out[16 * r2 + 4 * v + q] = msgs[16 * v:16 * v + 16, 128 * q:128 * q + 128]

        @pl.when(i > 0)
        def _():
            send(i - 1)

        return carry

    if ready is not None:
        ready()
    lax.fori_loop(0, 16, chunk, 0)
    send(15)
    own = pltpu.make_async_copy(out.at[me], h_ref.at[me], ls)
    own.start()
    w = pltpu.make_async_remote_copy(
        out.at[pl.ds(0, 255)], h_ref.at[pl.ds(0, 255)], ss, rs,
        device_id=(prow, col), device_id_type=MESH,
    )
    w.wait_recv()
    w.wait_send()
    own.wait()


def halo_scratch():
    return [
        pltpu.VMEM((512, 256), BF16),
        pltpu.VMEM((512, 512), BF16),
        pltpu.VMEM((DEVS, 16, 128), BF16),
        pltpu.SemaphoreType.DMA,
        pltpu.SemaphoreType.DMA,
        pltpu.SemaphoreType.DMA,
    ]


def normalize(z, total_gram, q_ref, p_ref):
    m = inverse_factor(unfold(total_gram) * (1.0 / NODES))
    put_wide(q_ref, nn(m, z))
    p_ref[...] = q_ref[...].astype(BF16)


def index_tables(w_ref, n_ref, l_ref, t_ref):
    wanted = jnp.concatenate([w_ref[pl.ds(q, 64, stride=4), :] for q in range(4)], axis=1)
    dest = lax.broadcasted_iota(jnp.int32, (64, 256), 1)
    group = lax.broadcasted_iota(jnp.int32, (64, 256), 0)
    spread = jnp.where(dest // 4 == group, n_ref[...].astype(F32), 0.0).astype(BF16)
    dest = lax.broadcasted_iota(jnp.int32, (256, 128), 0)
    lane = lax.broadcasted_iota(jnp.int32, (256, 128), 1)
    pick = jnp.where(lax.rem(dest, 4) == lane // 32, 1.0, 0.0).astype(BF16)
    live = jnp.dot(spread, pick, preferred_element_type=F32)
    slot = lax.rem(lax.broadcasted_iota(jnp.int32, (64, 128), 1), 32)
    l_ref[...] = lax.rem(wanted, 256)
    t_ref[...] = jnp.where(slot.astype(F32) < live, wanted // 256, -1)


def first_kernel(x_ref, w_ref, n_ref, q_ref, p_ref, h_ref, l_ref, t_ref, *scratch):
    greet()
    x = wide(x_ref)
    scratch[0][...] = fold(nt(x, x))
    greeted()

    def during():
        scratch[8][...] = swap_matrix()
        index_tables(w_ref, n_ref, l_ref, t_ref)

    g = total(scratch[:7], during)
    normalize(wide(x_ref), g, q_ref, p_ref)
    send_halo(q_ref, l_ref, t_ref, h_ref, scratch[7:])


def diagonal(g):
    i = lax.broadcasted_iota(jnp.int32, (BLK, BLK), 0)
    j = lax.broadcasted_iota(jnp.int32, (BLK, BLK), 1)
    return jnp.sum(jnp.where(i == j, g, 0.0), axis=1, keepdims=True)


def project_kernel(nb, *refs):
    y_ref, c_ref = refs[:2]
    basis = refs[2:2 + nb]
    z_ref, g_ref, ok_ref = refs[2 + nb:5 + nb]
    scratch = refs[5 + nb:]
    greet()
    scratch[0][...] = c_ref[...]
    greeted()
    c = total(scratch) * (1.0 / NODES)
    whole = unfold(c[32 * nb:])
    g = whole
    z = wide(y_ref)
    for i, b in enumerate(basis):
        part = unfold(c[32 * i:32 * i + 32])
        g = g - nt(part, part)
        z = z - nn(part, wide(b))
    put_wide(z_ref, z)
    g_ref[...] = fold(g)
    kept = jnp.min(diagonal(g) - 0.25 * diagonal(whole), axis=0, keepdims=True)
    ok_ref[...] = jnp.broadcast_to(jnp.where(kept > 0.0, 1, 0), (8, 128))


def fast_kernel(z_ref, g_ref, l_ref, t_ref, q_ref, p_ref, h_ref, sem, *scratch):
    greet_all()
    m = inverse_factor(unfold(g_ref[...]))
    scratch[1][...] = swap_matrix()
    greeted_all_first(sem)
    put_wide(q_ref, nn(m, wide(z_ref)))
    p_ref[...] = q_ref[...].astype(BF16)
    send_halo(q_ref, l_ref, t_ref, h_ref, scratch, lambda: greeted_all_second(sem))


def slow_kernel(z_ref, g_ref, l_ref, t_ref, q_ref, p_ref, h_ref, *scratch):
    greet()
    z = wide(z_ref)
    scratch[0][...] = fold(nt(z, z))
    scratch[8][...] = swap_matrix()
    greeted()
    g = total(scratch[:7])
    normalize(wide(z_ref), g, q_ref, p_ref)
    send_halo(q_ref, l_ref, t_ref, h_ref, scratch[7:])


def gram_kernel(z_ref, g_ref, o_ref, *scratch):
    greet()
    z = wide(z_ref)
    scratch[0][...] = fold(nt(z, z))
    greeted()
    o_ref[...] = total(scratch) * (1.0 / NODES)


def last_kernel(z_ref, g_ref, q0_ref, q1_ref, rot_ref, o_ref):
    rot = rot_ref[...]
    m = inverse_factor(unfold(g_ref[...]))
    tail = nn(rot[:, 128:192], m)
    o = nn(rot[:, 0:64], wide(q0_ref)) + nn(rot[:, 64:128], wide(q1_ref)) + nn(tail, wide(z_ref))
    put_wide(o_ref, o)


def apply_kernel(nb, *refs):
    rows, cols, count, values, p_ref, h_ref = refs[:6]
    basis = refs[6:6 + nb]
    y_ref, c_ref, src, acc, swap = refs[6 + nb:]
    n = count[0]
    nchunk = (n + CHUNK - 1) // CHUNK

    acc[...] = jnp.zeros_like(acc)
    src[0:RT] = p_ref[...]
    swap[...] = swap_matrix()

    def unpack(h, carry):
        parts = [
            jnp.concatenate([h_ref[32 * h + 4 * u + q] for q in range(4)], axis=1) for u in range(8)
        ]
        tiles = jnp.dot(jnp.concatenate(parts, axis=0), swap[...], preferred_element_type=F32).astype(BF16)
        for u in range(8):
            for g in range(4):
                src[RT + 8 * h + u, 16 * g:16 * g + 16, :] = tiles[16 * u:16 * u + 16, 128 * g:128 * g + 128]
        return carry

    lax.fori_loop(0, 8, unpack, 0)

    def step(c, carry):
        for u in range(CHUNK):
            k = c * CHUNK + u
            r = jnp.where(k < n, rows[k], RT)
            acc[r] += lax.dot_general(
                src[cols[k]], values[k], (((1,), (1,)), ((), ())), preferred_element_type=F32
            )
        return carry

    lax.fori_loop(0, nchunk, step, 0)
    y_ref[...] = acc[0:RT]
    y = wide(acc)
    c_ref[...] = jnp.concatenate([fold(nt(y, wide(b))) for b in basis] + [fold(nt(y, y))], axis=0)


def block(dtype):
    return jax.ShapeDtypeStruct((RT, BLK, TILE), dtype)


def remote(kernel, cid, outs, scratch, *operands):
    return pl.pallas_call(
        kernel,
        out_shape=outs,
        in_specs=[VMEM] * len(operands),
        out_specs=(VMEM,) * len(outs),
        scratch_shapes=scratch,
        cost_estimate=pl.CostEstimate(flops=20_000_000_000, bytes_accessed=100_000_000, transcendentals=0),
        compiler_params=pltpu.CompilerParams(
            collective_id=cid, has_side_effects=True, vmem_limit_bytes=24 * 1024 * 1024
        ),
    )(*operands)


def apply_graph(rows, cols, count, values, p, halo, basis):
    nb = len(basis)
    return pl.pallas_call(
        functools.partial(apply_kernel, nb),
        out_shape=(block(F32), jax.ShapeDtypeStruct((32 * nb + 32, 128), F32)),
        in_specs=[SMEM] * 3 + [VMEM] * (3 + nb),
        out_specs=(VMEM,) * 2,
        scratch_shapes=[
            pltpu.VMEM((80, BLK, TILE), BF16),
            pltpu.VMEM((RT + 1, BLK, TILE), F32),
            pltpu.VMEM((512, 512), BF16),
        ],
        compiler_params=pltpu.CompilerParams(vmem_limit_bytes=24 * 1024 * 1024),
    )(rows, cols, count, values, p, halo, *basis)


def body(start, values, rows, cols, count, send_rows, send_count, rotation):
    state = (block(F32), block(BF16), jax.ShapeDtypeStruct((DEVS, 16, 128), BF16))
    table = jax.ShapeDtypeStruct((64, 128), jnp.int32)
    q0, p, halo, lsel, tsel = remote(
        first_kernel, 1, state + (table, table), sum_scratch(32) + halo_scratch(), start, send_rows[0], send_count
    )
    y, c = apply_graph(rows, cols, count, values, p, halo, [q0])
    z, g, ok = project(2, y, c, [q0])

    def fast(z, g, l, t):
        return tuple(remote(fast_kernel, 3, state, [pltpu.SemaphoreType.REGULAR] + halo_scratch(), z, g, l, t))

    def slow(z, g, l, t):
        return tuple(remote(slow_kernel, 4, state, sum_scratch(32) + halo_scratch(), z, g, l, t))

    q1, p, halo = lax.cond(ok[0, 0] > 0, fast, slow, z, g, lsel, tsel)
    y, c = apply_graph(rows, cols, count, values, p, halo, [q0, q1])
    z, g, ok = project(5, y, c, [q0, q1])
    small = (jax.ShapeDtypeStruct((32, 128), F32),)
    g = lax.cond(
        ok[0, 0] > 0, lambda z, g: g, lambda z, g: remote(gram_kernel, 6, small, sum_scratch(32), z, g)[0], z, g
    )
    return pl.pallas_call(
        last_kernel,
        out_shape=block(F32),
        in_specs=[VMEM] * 5,
        out_specs=VMEM,
        compiler_params=pltpu.CompilerParams(vmem_limit_bytes=24 * 1024 * 1024),
    )(z, g, q0, q1, rotation.T)


def project(cid, y, c, basis):
    nb = len(basis)
    outs = (block(F32), jax.ShapeDtypeStruct((32, 128), F32), jax.ShapeDtypeStruct((8, 128), jnp.int32))
    return remote(functools.partial(project_kernel, nb), cid, outs, sum_scratch(32 * nb + 32), y, c, *basis)


def solution(mesh):
    spec = P(("row", "col"))
    return jax.shard_map(
        body,
        mesh=mesh,
        in_specs=(spec,) * 7 + (P(),),
        out_specs=spec,
        check_vma=False,
    )
```

```python
import functools

import jax
import jax.numpy as jnp
from jax import lax
from jax.experimental import pallas as pl
from jax.experimental.pallas import tpu as pltpu
from jax.sharding import PartitionSpec as P

MESH = pl.DeviceIdType.MESH
HIGHEST = lax.Precision.HIGHEST
F32 = jnp.float32
BF16 = jnp.bfloat16
RT = 16
BLK = 64
TILE = 128
DEVS = 256
NODES = 524288
CHUNK = 16
VMEM = pl.BlockSpec(memory_space=pltpu.VMEM)
SMEM = pl.BlockSpec(memory_space=pltpu.SMEM)


def place():
    row = lax.axis_index("row")
    col = lax.axis_index("col")
    return row, col, row + 1 - 2 * lax.rem(row, 2)


def greet():
    row, col, prow = place()
    bar = pltpu.get_barrier_semaphore()
    pl.semaphore_signal(bar, inc=1, device_id=(prow, col), device_id_type=MESH)

    def greet_xy(i, c):
        pl.semaphore_signal(bar, inc=1, device_id=(row, lax.rem(col + i, 16)), device_id_type=MESH)
        return c

    lax.fori_loop(1, 16, greet_xy, 0)

    def greet_z(i, c):
        pl.semaphore_signal(bar, inc=1, device_id=(lax.rem(row + 2 * i, 16), col), device_id_type=MESH)
        return c

    lax.fori_loop(1, 8, greet_z, 0)


def greeted():
    pl.semaphore_wait(pltpu.get_barrier_semaphore(), 23)


def greet_all():
    row, col, _ = place()
    bar = pltpu.get_barrier_semaphore()

    def one(i, c):
        pl.semaphore_signal(bar, inc=1, device_id=(row, lax.rem(col + i, 16)), device_id_type=MESH)
        pl.semaphore_signal(bar, inc=1, device_id=(lax.rem(row + i, 16), col), device_id_type=MESH)
        return c

    lax.fori_loop(1, 16, one, 0)


def greeted_all_first(sem):
    row, col, _ = place()
    pl.semaphore_wait(pltpu.get_barrier_semaphore(), 30)

    def one(i, c):
        pl.semaphore_signal(sem, inc=1, device_id=(lax.rem(row + i, 16), col), device_id_type=MESH)
        return c

    lax.fori_loop(1, 16, one, 0)


def greeted_all_second(sem):
    pl.semaphore_wait(sem, 15)


def sum_scratch(rows):
    half = rows // 2
    return [
        pltpu.VMEM((rows, 128), F32),
        pltpu.VMEM((half, 128), F32),
        pltpu.VMEM((16, half, 128), F32),
        pltpu.VMEM((8, half, 128), F32),
        pltpu.VMEM((rows, 128), F32),
        pltpu.SemaphoreType.DMA((4,)),
        pltpu.SemaphoreType.DMA((4,)),
    ]


def total(scratch, during=None):
    xbuf, pbuf, xybuf, zbuf, fin, ss, rs = scratch
    row, col, prow = place()
    core = lax.rem(row, 2)
    z = row // 2
    half = pbuf.shape[0]
    mine = pl.ds(pl.multiple_of(core * half, half), half)
    other = pl.ds(pl.multiple_of((1 - core) * half, half), half)
    cp = pltpu.make_async_remote_copy(
        xbuf.at[other], pbuf, ss.at[0], rs.at[0], device_id=(prow, col), device_id_type=MESH
    )
    cp.start()
    cp.wait()
    xybuf[col] = xbuf[mine, :] + pbuf[...]

    def send_xy(i, c):
        pltpu.make_async_remote_copy(
            xybuf.at[col], xybuf.at[col], ss.at[1], rs.at[1],
            device_id=(row, lax.rem(col + i, 16)), device_id_type=MESH,
        ).start()
        return c

    lax.fori_loop(1, 16, send_xy, 0)
    if during is not None:
        during()
    w = pltpu.make_async_remote_copy(
        xybuf.at[pl.ds(0, 15)], xybuf.at[pl.ds(0, 15)], ss.at[1], rs.at[1],
        device_id=(prow, col), device_id_type=MESH,
    )
    w.wait_recv()
    w.wait_send()
    zbuf[z] = jnp.sum(xybuf[...], axis=0)

    def send_z(i, c):
        pltpu.make_async_remote_copy(
            zbuf.at[z], zbuf.at[z], ss.at[2], rs.at[2],
            device_id=(lax.rem(row + 2 * i, 16), col), device_id_type=MESH,
        ).start()
        return c

    lax.fori_loop(1, 8, send_z, 0)
    w = pltpu.make_async_remote_copy(
        zbuf.at[pl.ds(0, 7)], zbuf.at[pl.ds(0, 7)], ss.at[2], rs.at[2],
        device_id=(prow, col), device_id_type=MESH,
    )
    w.wait_recv()
    w.wait_send()
    fin[mine, :] = jnp.sum(zbuf[...], axis=0)
    cp = pltpu.make_async_remote_copy(
        fin.at[mine], fin.at[mine], ss.at[3], rs.at[3], device_id=(prow, col), device_id_type=MESH
    )
    cp.start()
    cp.wait()
    return fin[...]


def nt(a, b):
    return lax.dot_general(a, b, (((1,), (1,)), ((), ())), precision=HIGHEST, preferred_element_type=F32)


def nn(a, b):
    return lax.dot_general(a, b, (((1,), (0,)), ((), ())), precision=HIGHEST, preferred_element_type=F32)


def wide(ref):
    return jnp.concatenate([ref[t] for t in range(RT)], axis=1)


def put_wide(ref, x):
    for t in range(RT):
        ref[t] = x[:, t * TILE:(t + 1) * TILE].astype(ref.dtype)


def fold(g):
    return jnp.concatenate([g[:32], g[32:]], axis=1)


def unfold(p):
    return jnp.concatenate([p[:, :64], p[:, 64:]], axis=0)


def inverse_factor(g):
    lane = lax.broadcasted_iota(jnp.int32, (8, 128), 1)
    sub = lax.broadcasted_iota(jnp.int32, (8, 128), 0)
    wide_g = jnp.concatenate([g, jnp.zeros((64, 64), F32)], axis=1)
    blocks = [
        jnp.where(lane == sub + (64 + 8 * b), 1.0, wide_g[8 * b:8 * b + 8]) for b in range(8)
    ]
    for j in range(0, 64, 2):
        jb, jr = divmod(j, 8)
        c1 = [jnp.broadcast_to(blocks[b][:, j:j + 1], (8, 128)) for b in range(jb, 8)]
        c2 = [jnp.broadcast_to(blocks[b][:, j + 1:j + 2], (8, 128)) for b in range(jb, 8)]
        r1 = blocks[jb][jr:jr + 1, :]
        ia = 1.0 / c1[0][jr:jr + 1, :]
        ratio = c1[0][jr + 1:jr + 2, :] * ia
        r2 = blocks[jb][jr + 1:jr + 2, :] - ratio * r1
        w2 = r2 / (c2[0][jr + 1:jr + 2, :] - ratio * c1[0][jr + 1:jr + 2, :])
        w1 = r1 * ia - ratio * w2
        for b in range(jb, 8):
            new = blocks[b] - (c1[b - jb] * w1 + c2[b - jb] * w2)
            if b == jb:
                new = jnp.where(sub > jr + 1, new, jnp.where(sub == jr + 1, r2, blocks[b]))
            blocks[b] = new
    out = []
    for b in range(8):
        d = jnp.sum(jnp.where(lane == sub + 8 * b, blocks[b], 0.0), axis=1, keepdims=True)
        out.append(blocks[b][:, 64:] / jnp.sqrt(d))
    return jnp.concatenate(out, axis=0)


def swap_matrix():
    k = lax.broadcasted_iota(jnp.int32, (512, 512), 0)
    n = lax.broadcasted_iota(jnp.int32, (512, 512), 1)
    goal = lax.rem(k // 32, 4) * 128 + (k // 128) * 32 + lax.rem(k, 32)
    return jnp.where(goal == n, 1.0, 0.0).astype(BF16)


def send_halo(q_ref, l_ref, t_ref, h_ref, scratch, ready=None):
    lhs, swap, out, ss, rs, ls = scratch
    row, col, prow = place()
    me = row * 16 + col
    for t in range(RT):
        lhs[64 * (t // 2):64 * (t // 2) + 64, 128 * (t % 2):128 * (t % 2) + 128] = q_ref[t].astype(BF16)
    node = lax.broadcasted_iota(jnp.int32, (256, 256), 0)

    core = lax.rem(row, 2)

    def target(i):
        k = i // 2
        away = (k + 1) // 2
        dz = jnp.where(lax.rem(k, 2) == 1, 4 - away, 4 + away)
        flip = lax.rem(i, 2)
        return 2 * lax.rem(row // 2 + dz, 8) + core + flip - 2 * core * flip

    def send(i):
        r2 = target(i)
        for u in range(16):
            c2 = lax.rem(col + 10 + u, 16)
            there = r2 * 16 + c2

            @pl.when(there != me)
            def _():
                pltpu.make_async_remote_copy(
                    out.at[there], h_ref.at[me], ss, rs, device_id=(r2, c2), device_id_type=MESH
                ).start()

    def chunk(i, carry):
        parts = []
        r2 = target(i)
        for e in range(2):
            c = 4 * r2 + 2 * e
            lsel = jnp.concatenate([l_ref[pl.ds(c, 1), :], l_ref[pl.ds(c + 1, 1), :]], axis=1)
            tsel = jnp.concatenate([t_ref[pl.ds(c, 1), :], t_ref[pl.ds(c + 1, 1), :]], axis=1)
            hot = jnp.where(node == lsel, 1.0, 0.0).astype(BF16)
            r = jnp.dot(lhs[...], hot, preferred_element_type=F32)
            acc = jnp.zeros((64, 256), F32)
            for t in range(8):
                acc = acc + jnp.where(tsel == t, r[64 * t:64 * t + 64], 0.0)
            acc = acc.astype(BF16)
            for h in range(2):
                parts.append(
                    jnp.concatenate([acc[16 * g:16 * g + 16, 128 * h:128 * h + 128] for g in range(4)], axis=1)
                )
        msgs = jnp.dot(jnp.concatenate(parts, axis=0), swap[...], preferred_element_type=F32).astype(BF16)
        for v in range(4):
            for q in range(4):
                out[16 * r2 + 4 * v + q] = msgs[16 * v:16 * v + 16, 128 * q:128 * q + 128]

        @pl.when(i > 0)
        def _():
            send(i - 1)

        return carry

    if ready is not None:
        ready()
    lax.fori_loop(0, 16, chunk, 0)
    send(15)
    own = pltpu.make_async_copy(out.at[me], h_ref.at[me], ls)
    own.start()
    w = pltpu.make_async_remote_copy(
        out.at[pl.ds(0, 255)], h_ref.at[pl.ds(0, 255)], ss, rs,
        device_id=(prow, col), device_id_type=MESH,
    )
    w.wait_recv()
    w.wait_send()
    own.wait()


def halo_scratch():
    return [
        pltpu.VMEM((512, 256), BF16),
        pltpu.VMEM((512, 512), BF16),
        pltpu.VMEM((DEVS, 16, 128), BF16),
        pltpu.SemaphoreType.DMA,
        pltpu.SemaphoreType.DMA,
        pltpu.SemaphoreType.DMA,
    ]


def normalize(z, total_gram, q_ref, p_ref):
    m = inverse_factor(unfold(total_gram) * (1.0 / NODES))
    put_wide(q_ref, nn(m, z))
    p_ref[...] = q_ref[...].astype(BF16)


def index_tables(w_ref, n_ref, l_ref, t_ref):
    wanted = jnp.concatenate([w_ref[pl.ds(q, 64, stride=4), :] for q in range(4)], axis=1)
    dest = lax.broadcasted_iota(jnp.int32, (64, 256), 1)
    group = lax.broadcasted_iota(jnp.int32, (64, 256), 0)
    spread = jnp.where(dest // 4 == group, n_ref[...].astype(F32), 0.0).astype(BF16)
    dest = lax.broadcasted_iota(jnp.int32, (256, 128), 0)
    lane = lax.broadcasted_iota(jnp.int32, (256, 128), 1)
    pick = jnp.where(lax.rem(dest, 4) == lane // 32, 1.0, 0.0).astype(BF16)
    live = jnp.dot(spread, pick, preferred_element_type=F32)
    slot = lax.rem(lax.broadcasted_iota(jnp.int32, (64, 128), 1), 32)
    l_ref[...] = lax.rem(wanted, 256)
    t_ref[...] = jnp.where(slot.astype(F32) < live, wanted // 256, -1)


def first_kernel(x_ref, w_ref, n_ref, q_ref, p_ref, h_ref, l_ref, t_ref, *scratch):
    greet()
    x = wide(x_ref)
    scratch[0][...] = fold(nt(x, x))
    greeted()

    def during():
        scratch[8][...] = swap_matrix()
        index_tables(w_ref, n_ref, l_ref, t_ref)

    g = total(scratch[:7], during)
    normalize(wide(x_ref), g, q_ref, p_ref)
    send_halo(q_ref, l_ref, t_ref, h_ref, scratch[7:])


def diagonal(g):
    i = lax.broadcasted_iota(jnp.int32, (BLK, BLK), 0)
    j = lax.broadcasted_iota(jnp.int32, (BLK, BLK), 1)
    return jnp.sum(jnp.where(i == j, g, 0.0), axis=1, keepdims=True)


def project_kernel(nb, *refs):
    y_ref, c_ref = refs[:2]
    basis = refs[2:2 + nb]
    rest = refs[2 + nb:]
    if nb == 2:
        rot_ref, z_ref, g_ref, ok_ref, part_ref = rest[:5]
        scratch = rest[5:]
    else:
        z_ref, g_ref, ok_ref = rest[:3]
        scratch = rest[3:]

    def during():
        if nb == 2:
            rot = rot_ref[...]
            put_wide(part_ref, nn(rot[:, 0:64], wide(basis[0])) + nn(rot[:, 64:128], wide(basis[1])))

    greet()
    scratch[0][...] = c_ref[...]
    greeted()
    c = total(scratch, during) * (1.0 / NODES)
    whole = unfold(c[32 * nb:])
    g = whole
    z = wide(y_ref)
    for i, b in enumerate(basis):
        part = unfold(c[32 * i:32 * i + 32])
        g = g - nt(part, part)
        z = z - nn(part, wide(b))
    put_wide(z_ref, z)
    g_ref[...] = fold(g)
    kept = jnp.min(diagonal(g) - 0.25 * diagonal(whole), axis=0, keepdims=True)
    ok_ref[...] = jnp.broadcast_to(jnp.where(kept > 0.0, 1, 0), (8, 128))


def fast_kernel(z_ref, g_ref, l_ref, t_ref, q_ref, p_ref, h_ref, sem, *scratch):
    greet_all()
    m = inverse_factor(unfold(g_ref[...]))
    scratch[1][...] = swap_matrix()
    greeted_all_first(sem)
    put_wide(q_ref, nn(m, wide(z_ref)))
    p_ref[...] = q_ref[...].astype(BF16)
    send_halo(q_ref, l_ref, t_ref, h_ref, scratch, lambda: greeted_all_second(sem))


def slow_kernel(z_ref, g_ref, l_ref, t_ref, q_ref, p_ref, h_ref, *scratch):
    greet()
    z = wide(z_ref)
    scratch[0][...] = fold(nt(z, z))
    scratch[8][...] = swap_matrix()
    greeted()
    g = total(scratch[:7])
    normalize(wide(z_ref), g, q_ref, p_ref)
    send_halo(q_ref, l_ref, t_ref, h_ref, scratch[7:])


def gram_kernel(z_ref, g_ref, o_ref, *scratch):
    greet()
    z = wide(z_ref)
    scratch[0][...] = fold(nt(z, z))
    greeted()
    o_ref[...] = total(scratch) * (1.0 / NODES)


def last_kernel(z_ref, g_ref, rot_ref, part_ref, o_ref):
    m = inverse_factor(unfold(g_ref[...]))
    tail = nn(rot_ref[:, 128:192], m)
    put_wide(o_ref, wide(part_ref) + nn(tail, wide(z_ref)))


def apply_kernel(nb, *refs):
    rows, cols, count, values, p_ref, h_ref = refs[:6]
    basis = refs[6:6 + nb]
    y_ref, c_ref, src, acc, swap, buf, sem = refs[6 + nb:]
    n = count[0]
    nchunk = (n + CHUNK - 1) // CHUNK

    def fetch(c):
        part = pl.ds(c * CHUNK, CHUNK)
        return pltpu.make_async_copy(values.at[part], buf.at[part], sem.at[c])

    def begin(c, carry):
        fetch(c).start()
        return carry

    lax.fori_loop(0, nchunk, begin, 0)
    acc[...] = jnp.zeros_like(acc)
    src[0:RT] = p_ref[...]
    swap[...] = swap_matrix()

    def unpack(h, carry):
        parts = [
            jnp.concatenate([h_ref[32 * h + 4 * u + q] for q in range(4)], axis=1) for u in range(8)
        ]
        tiles = jnp.dot(jnp.concatenate(parts, axis=0), swap[...], preferred_element_type=F32).astype(BF16)
        for u in range(8):
            for g in range(4):
                src[RT + 8 * h + u, 16 * g:16 * g + 16, :] = tiles[16 * u:16 * u + 16, 128 * g:128 * g + 128]
        return carry

    lax.fori_loop(0, 8, unpack, 0)

    def step(c, carry):
        fetch(c).wait()
        for u in range(CHUNK):
            k = c * CHUNK + u
            r = jnp.where(k < n, rows[k], RT)
            acc[r] += lax.dot_general(
                src[cols[k]], buf[k], (((1,), (1,)), ((), ())), preferred_element_type=F32
            )
        return carry

    lax.fori_loop(0, nchunk, step, 0)
    y_ref[...] = acc[0:RT]
    y = wide(acc)
    c_ref[...] = jnp.concatenate([fold(nt(y, wide(b))) for b in basis] + [fold(nt(y, y))], axis=0)


def block(dtype):
    return jax.ShapeDtypeStruct((RT, BLK, TILE), dtype)


def remote(kernel, cid, outs, scratch, *operands):
    return pl.pallas_call(
        kernel,
        out_shape=outs,
        in_specs=[VMEM] * len(operands),
        out_specs=(VMEM,) * len(outs),
        scratch_shapes=scratch,
        cost_estimate=pl.CostEstimate(flops=20_000_000_000, bytes_accessed=100_000_000, transcendentals=0),
        compiler_params=pltpu.CompilerParams(
            collective_id=cid, has_side_effects=True, vmem_limit_bytes=24 * 1024 * 1024
        ),
    )(*operands)


def apply_graph(rows, cols, count, values, p, halo, basis):
    nb = len(basis)
    return pl.pallas_call(
        functools.partial(apply_kernel, nb),
        out_shape=(block(F32), jax.ShapeDtypeStruct((32 * nb + 32, 128), F32)),
        in_specs=[SMEM] * 3 + [pl.BlockSpec(memory_space=pl.ANY)] + [VMEM] * (2 + nb),
        out_specs=(VMEM,) * 2,
        scratch_shapes=[
            pltpu.VMEM((80, BLK, TILE), BF16),
            pltpu.VMEM((RT + 1, BLK, TILE), F32),
            pltpu.VMEM((512, 512), BF16),
            pltpu.VMEM((DEVS, TILE, TILE), BF16),
            pltpu.SemaphoreType.DMA((DEVS // CHUNK,)),
        ],
        compiler_params=pltpu.CompilerParams(vmem_limit_bytes=24 * 1024 * 1024),
    )(rows, cols, count, values, p, halo, *basis)


def body(start, values, rows, cols, count, send_rows, send_count, rotation):
    state = (block(F32), block(BF16), jax.ShapeDtypeStruct((DEVS, 16, 128), BF16))
    values = pltpu.with_memory_space_constraint(values, pltpu.HBM)
    table = jax.ShapeDtypeStruct((64, 128), jnp.int32)
    q0, p, halo, lsel, tsel = remote(
        first_kernel, 1, state + (table, table), sum_scratch(32) + halo_scratch(), start, send_rows[0], send_count
    )
    y, c = apply_graph(rows, cols, count, values, p, halo, [q0])
    z, g, ok = project(2, y, c, [q0])

    def fast(z, g, l, t):
        return tuple(remote(fast_kernel, 3, state, [pltpu.SemaphoreType.REGULAR] + halo_scratch(), z, g, l, t))

    def slow(z, g, l, t):
        return tuple(remote(slow_kernel, 4, state, sum_scratch(32) + halo_scratch(), z, g, l, t))

    q1, p, halo = lax.cond(ok[0, 0] > 0, fast, slow, z, g, lsel, tsel)
    y, c = apply_graph(rows, cols, count, values, p, halo, [q0, q1])
    turned = rotation.T
    z, g, ok, part = project(5, y, c, [q0, q1], turned)
    small = (jax.ShapeDtypeStruct((32, 128), F32),)
    g = lax.cond(
        ok[0, 0] > 0, lambda z, g: g, lambda z, g: remote(gram_kernel, 6, small, sum_scratch(32), z, g)[0], z, g
    )
    return pl.pallas_call(
        last_kernel,
        out_shape=block(F32),
        in_specs=[VMEM] * 4,
        out_specs=VMEM,
        compiler_params=pltpu.CompilerParams(vmem_limit_bytes=24 * 1024 * 1024),
    )(z, g, turned, part)


def project(cid, y, c, basis, *more):
    nb = len(basis)
    outs = (block(F32), jax.ShapeDtypeStruct((32, 128), F32), jax.ShapeDtypeStruct((8, 128), jnp.int32))
    outs += (block(F32),) * len(more)
    return remote(functools.partial(project_kernel, nb), cid, outs, sum_scratch(32 * nb + 32), y, c, *basis, *more)


def solution(mesh):
    spec = P(("row", "col"))
    return jax.shard_map(
        body,
        mesh=mesh,
        in_specs=(spec,) * 7 + (P(),),
        out_specs=spec,
        check_vma=False,
    )
```
